32 devices in a mesh: rep: 2 (over x), seq: 16 (over z, y, core).
Axes of the slice: x: 2, y: 2, z: 4, core: 2. Of those that a mesh axis runs over, the one named last changes fastest.
Arguments:
- queries: bfloat16 [32, 32, 5120], P('seq', 'rep'), parts along dimension 1, may hold values from -4 to 4
- key_states: bfloat16 [32, 32, 5120], P('seq', 'rep'), parts along dimension 1, may hold values from -6 to 6
- value_states: bfloat16 [32, 32, 5120], P('seq', 'rep'), parts along dimension 1, may hold values from -6 to 6
- hidden: bfloat16 [32, 32, 5120], P('seq', 'rep'), parts along dimension 1, may hold values from -6 to 6
- residual_gate: float32 [32, 5120], P('rep'), parts along dimension 0, may hold values from 0.5 to 1.5
- head_shift: float32 [32, 5120], P('rep'), parts along dimension 0, may hold values from -3 to 3
- head_scale: float32 [32, 5120], P('rep'), parts along dimension 0, may hold values from -1.5 to 1.5
- head_weight: bfloat16 [5120, 64], replicated, may hold values from -0.078125 to 0.078125
- head_bias: float32 [64], replicated, may hold values from -3 to 3
- guidance: float32 [16], P('rep'), parts along dimension 0, may hold values from 3 to 7
- step_index: int32 [16], P('rep'), parts along dimension 0, may hold values from 0 to 9
- lengths: int32 [16], P('rep'), parts along dimension 0, may hold values from 1 to 32, 128 in all
- latent: float32 [32, 16, 64], P('seq', 'rep'), parts along dimension 1, may hold values from -6 to 6
- embed_weight: bfloat16 [64, 5120], replicated, may hold values from -0.75 to 0.75
- embed_bias: float32 [5120], replicated, may hold values from -3 to 3
- adapter_ids: int32 [16], P('rep'), parts along dimension 0, may hold values from 0 to 15
- adapter_down: bfloat16 [16, 5120, 64], P('seq'), may hold values from -0.078125 to 0.078125
- adapter_up: bfloat16 [16, 15360, 64], P('seq'), may hold values from -0.75 to 0.75
Outputs:
- velocity: float32 [32, 16, 64], P('seq', 'rep'), parts along dimension 1
- latent_next: float32 [32, 16, 64], P('seq', 'rep'), parts along dimension 1
- adapter_delta: bfloat16 [32, 16, 15360], P(None, 'rep', 'seq'), parts along dimension 1
The draws below stay inside these ranges and needn't reach their ends.
There are 2 independent parts, one for each index of `rep`. The reference program is written for one: setup_inputs(seed, part) draws one part's arguments, and reference() takes and returns one part's arrays. A program takes and returns all parts, laid end to end along the dimension named above; an argument that names none is the same for every part. Nothing has to cross between parts.
All inputs are finite; a program needn't handle non-finite values.
Results may differ from the reference program's by a relative error of at most 0.0066.
Values may be sent and summed in bfloat16 or wider, within the bound.
No kernel may reach another device: no remote copies, remote signals or barrier semaphores. Data moves between devices by JAX's collectives and lax.ppermute only.
A program may use at most 128 MiB of HBM per device.

```python
import math
import jax
import jax.numpy as jnp
import numpy as np
from jax import lax

WIDTH = 5120
HEADS = 40
HEAD_DIM = 128
PATCH_CH = 64
RANK = 64
REQUESTS = 8
STEPS = 10
SEQ_LEN = 32
STREAMS = 16
USERS = 16


def draw_queries(key, part):
    shape_all = (SEQ_LEN, STREAMS, WIDTH)
    base_vals = jnp.clip(jax.random.normal(jax.random.fold_in(key, 21), shape_all, jnp.float32), -4.0, 4.0)
    return base_vals.astype(jnp.bfloat16)


def draw_key_states(key, part):
    shape_all = (SEQ_LEN, STREAMS, WIDTH)
    base_vals = jnp.clip(jax.random.normal(jax.random.fold_in(key, 31), shape_all, jnp.float32), -4.0, 4.0)
    return base_vals.astype(jnp.bfloat16)


def touch_ends(values, stream_key, smallest, largest):
    index_at = [jax.random.randint(jax.random.fold_in(stream_key, axis), (), 0, length) for axis, length in enumerate(values.shape)]
    main_axis = values.shape.index(max(values.shape))
    beside = index_at[:main_axis] + [(index_at[main_axis] + 1) % values.shape[main_axis]] + index_at[main_axis + 1:]
    return values.at[tuple(index_at)].set(smallest).at[tuple(beside)].set(largest)


def shard_levels(stream_key, dims, split, low, top_value):
    gain, own = 1.0, jax.random.fold_in(stream_key, 6)
    for dim, shards_of in split:
        steps = jnp.exp(jax.random.uniform(jax.random.fold_in(own, dim), (shards_of,), jnp.float32, low / len(split), top_value / len(split)))
        gain = gain * jnp.repeat(steps, dims[dim] // shards_of).reshape([-1 if axis == dim else 1 for axis in range(len(dims))])
    return gain


def split_up(number_of, total, most, slope):
    loads = [(1 << 20) // math.isqrt(standing ** slope) + 1 for standing in range(2, number_of + 1)]
    surplus, counts = total - most - (number_of - 1), [1] * (number_of - 1)
    while surplus > 0:
        free = [i for i in range(number_of - 1) if counts[i] < most]
        pool, left = sum([loads[i] for i in free]), surplus
        for i in free:
            more = min(most - counts[i], max(1, left * loads[i] // pool), surplus)
            counts[i] = counts[i] + more
            surplus = surplus - more
    return np.array([most] + counts)


def uneven_parts(stream_key, amount, total, limit, lean):
    if amount == 2:
        one = jax.random.randint(stream_key, (), max(1, total - limit), min(limit, total - 1) + 1)
        return jnp.stack([one, total - one])
    sizes = jnp.asarray(split_up(amount, total, limit, lean), jnp.int32)
    couples = (amount - 1) // 2
    source_of, receiver = sizes[1:1 + 2 * couples:2], sizes[2:2 + 2 * couples:2]
    slack = jnp.minimum(source_of - 1, limit - receiver)
    moved = jax.random.randint(jax.random.fold_in(stream_key, 1), (couples,), 0, 1 << 20) % (slack + 1)
    sizes = sizes.at[1:1 + 2 * couples:2].set(source_of - moved).at[2:2 + 2 * couples:2].set(receiver + moved)
    return sizes[jax.random.permutation(jax.random.fold_in(stream_key, 2), amount)]


def gaussian(key, extent, scale, bound, shards=(), kind=jnp.bfloat16):
    factor_of = shard_levels(key, extent, shards, -0.22, 0.18) if shards else 1.0
    entries = jax.random.normal(key, extent, jnp.float32) * scale * factor_of
    return jnp.minimum(jnp.maximum(entries, -bound), bound).astype(kind)


def setup_inputs(seed: int = 0, part: int = 0) -> dict:
    splits = jax.random.split(jax.random.key(seed), 19)
    own_keys = jax.random.split(jax.random.fold_in(splits[18], part), 19)
    return {
        "queries": draw_queries(jax.random.fold_in(jax.random.fold_in(splits[18], part), 71), part),
        "key_states": draw_key_states(jax.random.fold_in(jax.random.fold_in(splits[18], part), 71), part),
        "value_states": gaussian(own_keys[2], (SEQ_LEN, STREAMS, WIDTH), 1.0, 6.0, ((0, 16),)),
        "hidden": gaussian(own_keys[3], (SEQ_LEN, STREAMS, WIDTH), 1.0, 6.0, ((0, 16),)),
        "residual_gate": jnp.clip(jax.random.uniform(own_keys[4], (STREAMS, WIDTH), jnp.float32, 0.5, 1.5), 0.5, 1.5),
        "head_shift": gaussian(own_keys[5], (STREAMS, WIDTH), 0.5, 3.0, (), jnp.float32),
        "head_scale": gaussian(own_keys[6], (STREAMS, WIDTH), 0.3, 1.5, (), jnp.float32),
        "head_weight": gaussian(splits[7], (WIDTH, PATCH_CH), WIDTH ** -0.5, 0.078125),
        "head_bias": gaussian(splits[8], (PATCH_CH,), 0.5, 3.0, (), jnp.float32),
        "guidance": jnp.clip(jax.random.uniform(own_keys[9], (REQUESTS,), jnp.float32, 3.0, 7.0), 3.0, 7.0),
        "step_index": touch_ends(jax.random.randint(own_keys[10], (REQUESTS,), 0, STEPS), jax.random.fold_in(own_keys[10], 1), 0, STEPS - 1).astype(jnp.int32),
        "lengths": uneven_parts(own_keys[11], REQUESTS, 4 * SEQ_LEN, SEQ_LEN, 2).astype(jnp.int32),
        "latent": gaussian(own_keys[12], (SEQ_LEN, REQUESTS, PATCH_CH), 1.0, 6.0, ((0, 16),), jnp.float32),
        "embed_weight": gaussian(splits[13], (PATCH_CH, WIDTH), PATCH_CH ** -0.5, 0.75),
        "embed_bias": gaussian(splits[14], (WIDTH,), 0.5, 3.0, (), jnp.float32),
        "adapter_ids": touch_ends(jax.random.randint(own_keys[15], (REQUESTS,), 0, USERS), jax.random.fold_in(own_keys[15], 1), 0, USERS - 1).astype(jnp.int32),
        "adapter_down": gaussian(splits[16], (USERS, WIDTH, RANK), WIDTH ** -0.5, 0.078125, ((0, 16),)),
        "adapter_up": gaussian(splits[17], (USERS, 3 * WIDTH, RANK), RANK ** -0.5, 0.75, ((0, 16),)),
    }


def noise_level(position):
    fraction = 1.0 - position / STEPS
    return 5.0 * fraction / (1.0 + 4.0 * fraction)

def layer_normed(rows):
    row_mean = lax.optimization_barrier(jnp.mean(rows, axis=-1, keepdims=True))
    centered = rows - row_mean
    row_var = lax.optimization_barrier(jnp.mean(centered * centered, axis=-1, keepdims=True))
    return centered * lax.rsqrt(row_var + 1e-06)

def reference(queries, key_states, value_states, hidden, residual_gate, head_shift, head_scale, head_weight, head_bias, guidance, step_index, lengths, latent, embed_weight, embed_bias, adapter_ids, adapter_down, adapter_up):
    item_count = STREAMS * HEADS
    score_scale = 1.0 / HEAD_DIM ** 0.5

    def as_items(states):
        return jnp.transpose(states.reshape(SEQ_LEN, item_count, HEAD_DIM), (1, 0, 2))
    item_stream = jnp.arange(item_count) // HEADS
    key_limit = lengths[item_stream % REQUESTS]

    def attend(operands):
        query_rows, key_rows, value_rows, key_bound = operands
        scores = jnp.einsum('qd,kd->qk', query_rows, key_rows, preferred_element_type=jnp.float32) * score_scale
        allowed = jnp.arange(SEQ_LEN)[None, :] < key_bound
        scores = jnp.where(allowed, scores, -jnp.inf)
        weights = jax.nn.softmax(scores, axis=-1).astype(jnp.bfloat16)
        return jnp.dot(weights, value_rows, preferred_element_type=jnp.float32).astype(jnp.bfloat16)
    attended = lax.map(attend, (as_items(queries), as_items(key_states), as_items(value_states), key_limit))
    attended = jnp.transpose(attended, (1, 0, 2)).reshape(SEQ_LEN, STREAMS, WIDTH)
    residual = hidden.astype(jnp.float32) + residual_gate[None, :, :] * attended.astype(jnp.float32)
    normed = (layer_normed(residual) * (1.0 + head_scale[None]) + head_shift[None]).astype(jnp.bfloat16)
    stream_velocity = jnp.dot(normed.reshape(-1, WIDTH), head_weight, preferred_element_type=jnp.float32)
    stream_velocity = stream_velocity.reshape(SEQ_LEN, STREAMS, PATCH_CH) + head_bias
    conditional = stream_velocity[:, :REQUESTS]
    unconditional = stream_velocity[:, REQUESTS:]
    velocity = unconditional + guidance[None, :, None] * (conditional - unconditional)
    sigma_now = noise_level(step_index.astype(jnp.float32))
    sigma_next = noise_level((step_index + 1).astype(jnp.float32))
    latent_next = latent + (sigma_next - sigma_now)[None, :, None] * velocity
    embedded = jnp.dot(latent_next.astype(jnp.bfloat16).reshape(-1, PATCH_CH), embed_weight, preferred_element_type=jnp.float32)
    embedded = embedded.reshape(SEQ_LEN, REQUESTS, WIDTH) + embed_bias
    block_input = layer_normed(embedded).astype(jnp.bfloat16)
    down_used = adapter_down[adapter_ids]
    up_used = adapter_up[adapter_ids]
    low_rank = jnp.einsum('lrd,rdk->lrk', block_input.astype(jnp.float32), down_used.astype(jnp.float32)).astype(jnp.bfloat16)
    adapter_delta = jnp.einsum('lrk,rck->lrc', low_rank.astype(jnp.float32), up_used.astype(jnp.float32)).astype(jnp.bfloat16)
    return (velocity, latent_next, adapter_delta)
```

```python
import functools

import jax
import jax.numpy as jnp
from jax import lax
from jax.experimental import pallas as pl
from jax.experimental.pallas import tpu as pltpu
from jax.sharding import PartitionSpec as P

HEADS = 40
HEAD_DIM = 128
REQUESTS = 8
STEPS = 10
LANES = 128
QUARTERS = 4
TABLE_ROWS = 72
VMEM_LIMIT = 56 << 20

NT = (((1,), (1,)), ((), ()))


def nt_dot(a, b):
    return lax.dot_general(a, b, NT, preferred_element_type=jnp.float32)


def prepare_kernel(
    place_ref,
    q_ref,
    k_ref,
    v_ref,
    h_ref,
    embed_ref,
    bias_ref,
    down_ref,
    up_ref,
    send_ref,
    gram_ref,
    *,
    devices,
    columns,
    half_tiles,
):
    row_count, stream_count, width = q_ref.shape
    quarter = width // QUARTERS
    tiles = quarter // LANES
    table_rows = half_tiles * TABLE_ROWS
    size = stream_count * 8
    to = lax.broadcasted_iota(jnp.int32, (size, size), 0)
    at = lax.broadcasted_iota(jnp.int32, (size, size), 1)
    same = (to // 8 == at % stream_count) & (to % 8 == at // stream_count)
    permutation = jnp.where(same, 1.0, 0.0).astype(jnp.bfloat16)
    for kind, ref in enumerate((q_ref, k_ref, v_ref, h_ref)):
        stacked = jnp.concatenate(
            [
                ref[token, :, part * quarter : (part + 1) * quarter]
                for part in range(QUARTERS)
                for token in range(row_count)
            ],
            axis=0,
        )
        moved = jnp.dot(permutation, stacked, preferred_element_type=jnp.float32)
        moved = moved.astype(jnp.bfloat16)
        for tile in range(tiles):
            first = table_rows + (kind * tiles + tile) * 8
            send_ref[:, first : first + 8, :] = moved[
                :, tile * LANES : (tile + 1) * LANES
            ].reshape(stream_count, 8, LANES)

    bias = bias_ref[...]
    high = bias.astype(jnp.bfloat16).astype(jnp.float32)
    middle = (bias - high).astype(jnp.bfloat16).astype(jnp.float32)
    low = bias - high - middle
    row = lax.broadcasted_iota(jnp.int32, (16, width), 0)
    extra = jnp.where(row == 0, high, jnp.where(row == 1, middle, jnp.where(row == 2, low, 0.0)))
    extra = jnp.where(row == 3, 1.0, extra).astype(jnp.bfloat16)
    rows = jnp.concatenate([embed_ref[...], extra], axis=0)
    raw = nt_dot(rows, down_ref[...])
    gram = nt_dot(rows, rows)
    ones_at = 67
    sums = gram[:, ones_at : ones_at + 1]
    centered = raw - sums * (1.0 / width) * raw[ones_at : ones_at + 1, :]
    gram_ref[...] = gram - sums * (1.0 / width) * gram[ones_at : ones_at + 1, :]
    bias_row = centered[64:65] + centered[65:66] + centered[66:67]
    tail = lax.broadcasted_iota(jnp.int32, (8, centered.shape[1]), 0)
    mixing = jnp.concatenate(
        [centered[:64], jnp.where(tail == 0, jnp.broadcast_to(bias_row, tail.shape), 0.0)], axis=0
    )
    mixing_high = mixing.astype(jnp.bfloat16)
    mixing_low = (mixing - mixing_high.astype(jnp.float32)).astype(jnp.bfloat16)
    mixing = jnp.concatenate([mixing_high, mixing_low], axis=1)

    half = half_tiles * LANES
    side = place_ref[1] * half
    for target in range(devices):
        start = columns * target // LANES * LANES
        part = up_ref[:, pl.ds(pl.multiple_of(start + side, LANES), half)]
        table = jnp.dot(
            mixing, jnp.concatenate([part, part], axis=0), preferred_element_type=jnp.float32
        ).astype(jnp.bfloat16)
        for tile in range(half_tiles):
            send_ref[target, tile * TABLE_ROWS : (tile + 1) * TABLE_ROWS, :] = table[
                :, tile * LANES : (tile + 1) * LANES
            ]


def select_kernel(ids_ref, table_ref, out_ref):
    out_ref[...] = table_ref[...]


def group_sum(x):
    grouped = x.reshape(x.shape[0] // 8, 8, x.shape[1])
    grouped = grouped + pltpu.roll(grouped, 2, 1)
    grouped = grouped + pltpu.roll(grouped, 4, 1)
    return grouped.reshape(x.shape)


def attend_kernel(
    place_ref,
    lengths_ref,
    got_ref,
    gate_ref,
    shift_ref,
    scale_ref,
    weight_ref,
    bias_ref,
    latent_ref,
    out_ref,
    residual_ref,
    pick_ref,
    *,
    table_rows,
):
    devices = got_ref.shape[0]
    width = gate_ref.shape[1]
    quarter = width // QUARTERS
    tiles = quarter // LANES
    size = devices * 8
    mine = place_ref[0]
    limit = lengths_ref[mine % REQUESTS]
    score_scale = 1.0 / HEAD_DIM**0.5

    row = lax.broadcasted_iota(jnp.int32, (size, size), 0)
    column = lax.broadcasted_iota(jnp.int32, (size, size), 1)
    key_token = column // 8 * 2 + column % 2
    allowed = (row % 8 // 2 == column % 8 // 2) & (key_token < limit)
    part_of_row = lax.broadcasted_iota(jnp.int32, (8, LANES), 0) // 2

    def own_row(ref):
        block = ref[pl.ds(pl.multiple_of(mine // 8 * 8, 8), 8), :]
        return pltpu.roll(block, (8 - mine % 8) % 8, 0)[0:1]

    gate, shift, scale = own_row(gate_ref), own_row(shift_ref), own_row(scale_ref)

    def per_row(values, tile):
        value = jnp.zeros((8, LANES), jnp.float32)
        for part in range(QUARTERS):
            first = part * quarter + tile * LANES
            piece = values[:, first : first + LANES]
            value = jnp.where(part_of_row == part, jnp.broadcast_to(piece, (8, LANES)), value)
        return value

    def widened(value):
        return jnp.broadcast_to(value[None], (devices, 8, LANES)).reshape(size, LANES)

    total = jnp.zeros((size, LANES), jnp.float32)
    for tile in range(tiles):
        q, k, v, h = [
            got_ref[
                :,
                table_rows + (kind * tiles + tile) * 8 : table_rows + (kind * tiles + tile) * 8 + 8,
                :,
            ].reshape(size, LANES)
            for kind in range(4)
        ]
        scores = jnp.where(allowed, nt_dot(q, k) * score_scale, -jnp.inf)
        peak = jnp.max(scores, axis=-1, keepdims=True)
        raised = jnp.exp(scores - peak)
        weights = raised / jnp.sum(raised, axis=-1, keepdims=True)
        attended = jnp.dot(
            weights.astype(jnp.bfloat16), v, preferred_element_type=jnp.float32
        ).astype(jnp.bfloat16)
        residual = h.astype(jnp.float32) + widened(per_row(gate, tile)) * attended.astype(
            jnp.float32
        )
        residual_ref[tile] = residual
        total = total + residual
    mean = jnp.sum(group_sum(total), axis=-1, keepdims=True) * (1.0 / width)
    total = jnp.zeros((size, LANES), jnp.float32)
    for tile in range(tiles):
        centered = residual_ref[tile] - mean
        residual_ref[tile] = centered
        total = total + centered * centered
    variance = jnp.sum(group_sum(total), axis=-1, keepdims=True) * (1.0 / width)
    inverse = lax.rsqrt(variance + 1e-06)
    channels = weight_ref.shape[0]
    product = jnp.zeros((size, QUARTERS * channels), jnp.float32)
    for tile in range(tiles):
        normed = residual_ref[tile] * inverse * widened(
            1.0 + per_row(scale, tile)
        ) + widened(per_row(shift, tile))
        weight = jnp.concatenate(
            [
                weight_ref[:, part * quarter + tile * LANES : part * quarter + (tile + 1) * LANES]
                for part in range(QUARTERS)
            ],
            axis=0,
        )
        product = product + nt_dot(normed.astype(jnp.bfloat16), weight)
    row = lax.broadcasted_iota(jnp.int32, product.shape, 0)
    column = lax.broadcasted_iota(jnp.int32, product.shape, 1)
    product = jnp.where(row % 8 // 2 == column // channels, product, 0.0)
    product = group_sum(product[:, :LANES] + product[:, LANES:])
    product = product + pltpu.roll(product, channels, 1)
    bias = bias_ref[...]
    product = product + jnp.concatenate([bias, bias], axis=1)
    pick_ref[...] = product
    first_token = pick_ref[pl.ds(0, devices, stride=8), :]
    second_token = pick_ref[pl.ds(1, devices, stride=8), :]
    lane = lax.broadcasted_iota(jnp.int32, (devices, LANES), 1)
    stream_velocity = jnp.where(lane < channels, first_token, second_token)
    latent = jnp.concatenate([latent_ref[0], latent_ref[1]], axis=1)
    block = jnp.concatenate([stream_velocity, latent], axis=0)
    out_ref[...] = jnp.broadcast_to(block[None], out_ref.shape)


def finish_kernel(
    place_ref,
    ids_ref,
    got_ref,
    guidance_ref,
    step_ref,
    gram_ref,
    near_ref,
    far_ref,
    velocity_ref,
    latent_ref,
    delta_ref,
    velocity_all,
    latent_all,
    product_ref,
    *,
    devices,
    columns,
    half_tiles,
):
    block = devices + REQUESTS
    guidance = guidance_ref[...]
    step = step_ref[...]
    lane = lax.broadcasted_iota(jnp.int32, (REQUESTS, LANES), 1)
    channels = LANES // 2
    pieces = []
    for source in range(devices):
        conditional = got_ref[pl.ds(source, REQUESTS, stride=block), :]
        unconditional = got_ref[pl.ds(REQUESTS * block + source, REQUESTS, stride=block), :]
        velocity = unconditional + guidance * (conditional - unconditional)
        first = source * block + devices
        latent_next = got_ref[first : first + REQUESTS, :] + step * velocity
        velocity_all[source] = velocity
        latent_all[source] = latent_next
        tail = jnp.where(lane < channels + 3, 1.0, 0.0)
        pieces.append(jnp.where(lane < channels, latent_next, tail))
        pieces.append(jnp.where(lane < channels, pltpu.roll(latent_next, channels, 1), tail))
    mine = place_ref[0]
    velocity = velocity_all[mine]
    latent_next = latent_all[mine]
    velocity_ref[0] = velocity[:, :channels]
    velocity_ref[1] = velocity[:, channels:]
    latent_ref[0] = latent_next[:, :channels]
    latent_ref[1] = latent_next[:, channels:]

    rounded = jnp.concatenate(pieces, axis=0).astype(jnp.bfloat16)
    rows = rounded.shape[0]
    exact = rounded.astype(jnp.float32)
    used = gram_ref.shape[0]
    image = jnp.dot(
        exact[:, :used],
        gram_ref[...],
        precision=lax.Precision.HIGHEST,
        preferred_element_type=jnp.float32,
    )
    spread = jnp.sum(image * exact[:, :used], axis=-1, keepdims=True)
    inverse = lax.rsqrt(spread * (1.0 / (HEADS * HEAD_DIM)) + 1e-06)

    request_of_row = lax.broadcasted_iota(jnp.int32, (rows, TABLE_ROWS), 0) % REQUESTS
    left = jnp.concatenate(
        [
            jnp.where(request_of_row == request, exact[:, :TABLE_ROWS], 0.0)
            for request in range(REQUESTS)
        ],
        axis=1,
    ).astype(jnp.bfloat16)
    half = half_tiles * LANES
    side = place_ref[1]
    for which, take in (
        (side, lambda request: near_ref[ids_ref[request]]),
        (1 - side, lambda request: far_ref[request]),
    ):
        tables = [take(request) for request in range(REQUESTS)]
        right = jnp.concatenate(
            [
                jnp.concatenate(
                    [table[tile * TABLE_ROWS : (tile + 1) * TABLE_ROWS] for table in tables], axis=0
                )
                for tile in range(half_tiles)
            ],
            axis=1,
        )
        product = jnp.dot(left, right, preferred_element_type=jnp.float32) * inverse
        product_ref[:, pl.ds(pl.multiple_of(which * half, LANES), half)] = product
    shape = delta_ref.shape
    offsets = sorted({columns * target % LANES for target in range(devices)})
    own = columns * mine % LANES
    for offset in offsets:

        @pl.when(own == offset)
        def _(offset=offset):
            kept = product_ref[:, offset : offset + columns]
            delta_ref[...] = kept.astype(jnp.bfloat16).reshape(shape)


def broadcast(value, axis, source):
    kept = jnp.where(lax.axis_index(axis) == source, value, 0).astype(value.dtype)
    return lax.psum(kept, axis)


def noise_level(position):
    fraction = 1.0 - position / STEPS
    return 5.0 * fraction / (1.0 + 4.0 * fraction)


def layer_normed(rows):
    row_mean = jnp.mean(rows, axis=-1, keepdims=True)
    centered = rows - row_mean
    row_var = jnp.mean(centered * centered, axis=-1, keepdims=True)
    return centered * lax.rsqrt(row_var + 1e-06)


def many_per_stream(
    queries,
    key_states,
    value_states,
    hidden,
    residual_gate,
    head_shift,
    head_scale,
    head_weight,
    head_bias,
    guidance,
    step_index,
    lengths,
    latent,
    embed_weight,
    embed_bias,
    adapter_ids,
    adapter_down,
    adapter_up,
):
    row_count, stream_count, feature_width = queries.shape
    axis_devices = lax.axis_size("seq")
    full_length = row_count * axis_devices
    item_count = stream_count * feature_width // HEAD_DIM
    local_items = item_count // axis_devices
    score_scale = 1.0 / HEAD_DIM**0.5

    def as_items(states):
        return states.reshape(row_count, item_count, HEAD_DIM)

    query_heads, key_heads, value_heads = (
        lax.all_to_all(as_items(queries), "seq", split_axis=1, concat_axis=0, tiled=True),
        lax.all_to_all(as_items(key_states), "seq", split_axis=1, concat_axis=0, tiled=True),
        lax.all_to_all(as_items(value_states), "seq", split_axis=1, concat_axis=0, tiled=True),
    )
    first_item = lax.axis_index("seq") * local_items
    item_request = (first_item + jnp.arange(local_items)) // HEADS % REQUESTS
    selector = (item_request[:, None] == jnp.arange(REQUESTS)[None, :]).astype(jnp.int32)
    key_limit = jnp.sum(selector * lengths[None, :], axis=1)

    def attend(operands):
        query_rows, key_rows, value_rows, key_bound = operands
        scores = (
            jnp.einsum("qd,kd->qk", query_rows, key_rows, preferred_element_type=jnp.float32)
            * score_scale
        )
        allowed = jnp.arange(full_length)[None, :] < key_bound
        scores = jnp.where(allowed, scores, -jnp.inf)
        weights = jax.nn.softmax(scores, axis=-1).astype(jnp.bfloat16)
        return jnp.dot(weights, value_rows, preferred_element_type=jnp.float32).astype(jnp.bfloat16)

    attended_items = lax.map(
        attend,
        (
            jnp.moveaxis(query_heads, 1, 0),
            jnp.moveaxis(key_heads, 1, 0),
            jnp.moveaxis(value_heads, 1, 0),
            key_limit,
        ),
    )
    returned = lax.all_to_all(
        jnp.moveaxis(attended_items, 0, 1), "seq", split_axis=0, concat_axis=1, tiled=True
    )
    attended = returned.reshape(row_count, stream_count, feature_width)
    residual = hidden.astype(jnp.float32) + residual_gate[None, :, :] * attended.astype(jnp.float32)
    normed = (layer_normed(residual) * (1.0 + head_scale[None]) + head_shift[None]).astype(
        jnp.bfloat16
    )
    stream_velocity = jnp.dot(
        normed.reshape(-1, feature_width), head_weight, preferred_element_type=jnp.float32
    )
    stream_velocity = stream_velocity.reshape(row_count, stream_count, -1) + head_bias
    conditional = stream_velocity[:, :REQUESTS]
    unconditional = stream_velocity[:, REQUESTS:]
    velocity = unconditional + guidance[None, :, None] * (conditional - unconditional)
    sigma_now = noise_level(step_index.astype(jnp.float32))
    sigma_next = noise_level((step_index + 1).astype(jnp.float32))
    latent_next = latent + (sigma_next - sigma_now)[None, :, None] * velocity
    latent_rounded = latent_next.astype(jnp.bfloat16)
    held_slots = adapter_down.shape[0]
    embedded = jnp.dot(
        latent_rounded.reshape(row_count * REQUESTS, -1),
        embed_weight,
        preferred_element_type=jnp.float32,
    )
    embedded = embedded.reshape(row_count, REQUESTS, feature_width) + embed_bias
    block_input = layer_normed(embedded).astype(jnp.bfloat16)
    up_parts = lax.all_to_all(adapter_up, "seq", split_axis=1, concat_axis=0, tiled=True)
    user_count = up_parts.shape[0]
    chooser = (adapter_ids[:, None] == jnp.arange(user_count)[None, :]).astype(jnp.bfloat16)
    up_used = jnp.einsum(
        "ru,uck->rck", chooser, up_parts, preferred_element_type=jnp.float32
    ).astype(jnp.bfloat16)
    down_list = []
    for request in range(REQUESTS):
        owner_device = adapter_ids[request] // held_slots
        owner_slot = adapter_ids[request] % held_slots
        own_down = lax.dynamic_index_in_dim(adapter_down, owner_slot, 0, keepdims=False)
        whole_down = broadcast(own_down, "seq", owner_device)
        down_list.append(whole_down)
    down_used = jnp.stack(down_list, axis=0)
    low_rank = jnp.einsum(
        "lrd,rdk->lrk", block_input, down_used, preferred_element_type=jnp.float32
    ).astype(jnp.bfloat16)
    low_rank_all = lax.all_gather(low_rank, "seq", axis=0, tiled=True)
    adapter_delta = jnp.einsum(
        "lrk,rck->lrc", low_rank_all, up_used, preferred_element_type=jnp.float32
    ).astype(jnp.bfloat16)
    return (velocity, latent_next, adapter_delta)


def whole(shape):
    return pl.BlockSpec(shape, lambda *_: (0,) * len(shape))


def one_stream_each(
    queries,
    key_states,
    value_states,
    hidden,
    residual_gate,
    head_shift,
    head_scale,
    head_weight,
    head_bias,
    guidance,
    step_index,
    lengths,
    latent,
    embed_weight,
    embed_bias,
    adapter_ids,
    adapter_down,
    adapter_up,
):
    devices = lax.axis_size("seq")
    row_count, stream_count, width = queries.shape
    columns = adapter_up.shape[1] // devices
    half_tiles = window_tiles(columns, devices) // 2
    table_rows = half_tiles * TABLE_ROWS
    send_rows = table_rows + 4 * (width // QUARTERS // LANES) * 8
    place = jnp.stack([lax.axis_index("seq"), lax.axis_index("rep")]).astype(jnp.int32)
    swap = [(0, 1), (1, 0)]
    other_ids = lax.ppermute(adapter_ids, "rep", swap)
    smem = pl.BlockSpec(memory_space=pltpu.SMEM)
    vmem = pl.BlockSpec(memory_space=pltpu.VMEM)
    params = pltpu.CompilerParams(vmem_limit_bytes=VMEM_LIMIT)

    send, gram = pl.pallas_call(
        functools.partial(
            prepare_kernel, devices=devices, columns=columns, half_tiles=half_tiles
        ),
        out_shape=(
            jax.ShapeDtypeStruct((devices, send_rows, LANES), jnp.bfloat16),
            jax.ShapeDtypeStruct((80, 80), jnp.float32),
        ),
        in_specs=[smem] + [vmem] * 8,
        out_specs=(vmem, vmem),
        compiler_params=params,
        name="prepare",
    )(
        place,
        queries,
        key_states,
        value_states,
        hidden,
        embed_weight,
        embed_bias[None, :],
        adapter_down[0].T,
        adapter_up[0].T,
    )
    got = lax.all_to_all(send, "seq", split_axis=0, concat_axis=0, tiled=True)

    chosen = pl.pallas_call(
        select_kernel,
        out_shape=jax.ShapeDtypeStruct((REQUESTS, table_rows, LANES), jnp.bfloat16),
        grid_spec=pltpu.PrefetchScalarGridSpec(
            num_scalar_prefetch=1,
            grid=(REQUESTS,),
            in_specs=[pl.BlockSpec((1, table_rows, LANES), lambda r, ids: (ids[r], 0, 0))],
            out_specs=pl.BlockSpec((1, table_rows, LANES), lambda r, ids: (r, 0, 0)),
        ),
        name="choose",
    )(other_ids, got)
    far = lax.ppermute(chosen, "rep", swap)

    payload_rows = devices + REQUESTS
    payload = pl.pallas_call(
        functools.partial(attend_kernel, table_rows=table_rows),
        out_shape=jax.ShapeDtypeStruct((devices, payload_rows, LANES), jnp.float32),
        in_specs=[smem, smem] + [vmem] * 7,
        out_specs=vmem,
        scratch_shapes=[
            pltpu.VMEM((width // QUARTERS // LANES, devices * 8, LANES), jnp.float32),
            pltpu.VMEM((devices * 8, LANES), jnp.float32),
        ],
        compiler_params=params,
        name="attend",
        cost_estimate=pl.CostEstimate(
            flops=10**9, bytes_accessed=4 * 10**6, transcendentals=2 * 10**5
        ),
    )(
        place,
        lengths,
        got,
        residual_gate,
        head_shift,
        head_scale,
        head_weight.T,
        head_bias[None, :],
        latent,
    )
    shared = lax.all_to_all(payload, "seq", split_axis=0, concat_axis=0, tiled=True)

    sigma_now = noise_level(step_index.astype(jnp.float32))
    sigma_next = noise_level((step_index + 1).astype(jnp.float32))
    across = (REQUESTS, LANES)
    return pl.pallas_call(
        functools.partial(finish_kernel, devices=devices, columns=columns, half_tiles=half_tiles),
        out_shape=(
            jax.ShapeDtypeStruct(latent.shape, jnp.float32),
            jax.ShapeDtypeStruct(latent.shape, jnp.float32),
            jax.ShapeDtypeStruct((row_count * devices, REQUESTS, columns), jnp.bfloat16),
        ),
        in_specs=[smem, smem] + [vmem] * 6,
        out_specs=(vmem, vmem, vmem),
        scratch_shapes=[
            pltpu.VMEM((devices,) + across, jnp.float32),
            pltpu.VMEM((devices,) + across, jnp.float32),
            pltpu.VMEM((row_count * devices * REQUESTS, 2 * half_tiles * LANES), jnp.float32),
        ],
        compiler_params=params,
        name="finish",
    )(
        place,
        adapter_ids,
        shared.reshape(devices * payload_rows, LANES),
        jnp.broadcast_to(guidance[:, None], across),
        jnp.broadcast_to((sigma_next - sigma_now)[:, None], across),
        gram,
        got,
        far,
    )


def window_tiles(columns, devices):
    most = max(
        pl.cdiv(columns * (d + 1), LANES) - columns * d // LANES for d in range(devices)
    )
    return (most + 1) // 2 * 2


def shards(*operands):
    queries, held, table = operands[0], operands[16], operands[17]
    row_count, stream_count, width = queries.shape
    devices = lax.axis_size("seq")
    columns = table.shape[1] // devices
    fits = (
        stream_count == devices
        and row_count == 2
        and held.shape[0] == 1
        and held.shape[2] == LANES // 2
        and lax.axis_size("rep") == 2
        and width % (QUARTERS * LANES) == 0
        and all(
            columns * d // LANES + window_tiles(columns, devices) <= table.shape[1] // LANES
            for d in range(devices)
        )
    )
    return one_stream_each(*operands) if fits else many_per_stream(*operands)


def solution(mesh):
    placed = (
        P("seq", "rep", None),
        P("seq", "rep", None),
        P("seq", "rep", None),
        P("seq", "rep", None),
        P("rep", None),
        P("rep", None),
        P("rep", None),
        P(),
        P(),
        P("rep"),
        P("rep"),
        P("rep"),
        P("seq", "rep", None),
        P(),
        P(),
        P("rep"),
        P("seq", None, None),
        P("seq", None, None),
    )
    return jax.shard_map(
        shards,
        mesh=mesh,
        in_specs=placed,
        out_specs=(P("seq", "rep", None), P("seq", "rep", None), P(None, "rep", "seq")),
        check_vma=False,
    )
```

```python
import functools

import jax
import jax.numpy as jnp
from jax import lax
from jax.experimental import pallas as pl
from jax.experimental.pallas import tpu as pltpu
from jax.sharding import PartitionSpec as P

HEADS = 40
HEAD_DIM = 128
REQUESTS = 8
STEPS = 10
LANES = 128
QUARTERS = 4
TABLE_ROWS = 72
VMEM_LIMIT = 20 << 20
PREPARE_VMEM_LIMIT = 56 << 20

NT = (((1,), (1,)), ((), ()))


def nt_dot(a, b):
    return lax.dot_general(a, b, NT, preferred_element_type=jnp.float32)


def prepare_kernel(*refs, devices, columns, half_tiles):
    sources, (send_ref, gram_ref), held, sems = refs[:8], refs[8:10], refs[10:18], refs[18]
    copies = [
        pltpu.make_async_copy(source, target, sems.at[index])
        for index, (source, target) in enumerate(zip(sources, held))
    ]
    for copy in copies:
        copy.start()
    q_ref, k_ref, v_ref, h_ref, embed_ref, bias_ref, down_ref, up_ref = held
    row_count, stream_count, width = q_ref.shape
    quarter = width // QUARTERS
    tiles = quarter // LANES
    table_rows = half_tiles * TABLE_ROWS
    size = stream_count * 8
    to = lax.broadcasted_iota(jnp.int32, (size, size), 0)
    at = lax.broadcasted_iota(jnp.int32, (size, size), 1)
    same = (to // 8 == at % stream_count) & (to % 8 == at // stream_count)
    permutation = jnp.where(same, 1.0, 0.0).astype(jnp.bfloat16)
    for kind, ref in enumerate((q_ref, k_ref, v_ref, h_ref)):
        copies[kind].wait()
        stacked = jnp.concatenate(
            [
                ref[token, :, part * quarter : (part + 1) * quarter]
                for part in range(QUARTERS)
                for token in range(row_count)
            ],
            axis=0,
        )
        moved = jnp.dot(permutation, stacked, preferred_element_type=jnp.float32)
        moved = moved.astype(jnp.bfloat16)
        for tile in range(tiles):
            first = table_rows + (kind * tiles + tile) * 8
            send_ref[:, first : first + 8, :] = moved[
                :, tile * LANES : (tile + 1) * LANES
            ].reshape(stream_count, 8, LANES)

    for copy in copies[4:7]:
        copy.wait()
    bias = bias_ref[...]
    high = bias.astype(jnp.bfloat16).astype(jnp.float32)
    middle = (bias - high).astype(jnp.bfloat16).astype(jnp.float32)
    low = bias - high - middle
    row = lax.broadcasted_iota(jnp.int32, (16, width), 0)
    extra = jnp.where(row == 0, high, jnp.where(row == 1, middle, jnp.where(row == 2, low, 0.0)))
    extra = jnp.where(row == 3, 1.0, extra).astype(jnp.bfloat16)
    rows = jnp.concatenate([embed_ref[...], extra], axis=0)
    raw = nt_dot(rows, down_ref[...])
    gram = nt_dot(rows, rows)
    ones_at = 67
    sums = gram[:, ones_at : ones_at + 1]
    centered = raw - sums * (1.0 / width) * raw[ones_at : ones_at + 1, :]
    gram_ref[...] = gram - sums * (1.0 / width) * gram[ones_at : ones_at + 1, :]
    bias_row = centered[64:65] + centered[65:66] + centered[66:67]
    tail = lax.broadcasted_iota(jnp.int32, (8, centered.shape[1]), 0)
    mixing = jnp.concatenate(
        [centered[:64], jnp.where(tail == 0, jnp.broadcast_to(bias_row, tail.shape), 0.0)], axis=0
    )
    mixing_high = mixing.astype(jnp.bfloat16)
    mixing_low = (mixing - mixing_high.astype(jnp.float32)).astype(jnp.bfloat16)
    mixing = jnp.concatenate([mixing_high, mixing_low], axis=1)

    half = half_tiles * LANES
    side = lax.axis_index("rep") * half
    copies[7].wait()
    for target in range(devices):
        start = columns * target // LANES * LANES
        part = up_ref[:, pl.ds(pl.multiple_of(start + side, LANES), half)]
        table = jnp.dot(
            mixing, jnp.concatenate([part, part], axis=0), preferred_element_type=jnp.float32
        ).astype(jnp.bfloat16)
        for tile in range(half_tiles):
            send_ref[target, tile * TABLE_ROWS : (tile + 1) * TABLE_ROWS, :] = table[
                :, tile * LANES : (tile + 1) * LANES
            ]


def choose_kernel(ids_ref, got_ref, out_ref, sems):
    count = out_ref.shape[1]
    copies = [
        pltpu.make_async_copy(
            got_ref.at[ids_ref[request], 0:count],
            out_ref.at[request],
            sems.at[request],
        )
        for request in range(REQUESTS)
    ]
    for copy in copies:
        copy.start()
    for copy in copies:
        copy.wait()


def group_sum(x):
    grouped = x.reshape(x.shape[0] // 8, 8, x.shape[1])
    grouped = grouped + pltpu.roll(grouped, 2, 1)
    grouped = grouped + pltpu.roll(grouped, 4, 1)
    return grouped.reshape(x.shape)


def modulate_kernel(gate_ref, shift_ref, scale_ref, weight_ref, rows_ref, head_ref):
    width = gate_ref.shape[1]
    quarter = width // QUARTERS
    mine = lax.axis_index("seq")
    part_of_row = lax.broadcasted_iota(jnp.int32, (8, quarter), 0) // 2
    for index, ref in enumerate((gate_ref, shift_ref, scale_ref)):
        block = ref[pl.ds(pl.multiple_of(mine // 8 * 8, 8), 8), :]
        row = pltpu.roll(block, (8 - mine % 8) % 8, 0)[0:1]
        value = jnp.zeros((8, quarter), jnp.float32)
        for part in range(QUARTERS):
            piece = row[:, part * quarter : (part + 1) * quarter]
            value = jnp.where(part_of_row == part, jnp.broadcast_to(piece, value.shape), value)
        rows_ref[index] = value
    channels = weight_ref.shape[0]
    for part in range(QUARTERS):
        head_ref[part * channels : (part + 1) * channels, :] = weight_ref[
            :, part * quarter : (part + 1) * quarter
        ]


def attend_kernel(
    lengths_ref,
    got_ref,
    rows_ref,
    head_ref,
    bias_ref,
    latent_ref,
    out_ref,
    residual_ref,
    pick_ref,
    *,
    table_rows,
):
    devices = got_ref.shape[0]
    quarter = rows_ref.shape[2]
    width = quarter * QUARTERS
    tiles = quarter // LANES
    size = devices * 8
    limit = lengths_ref[lax.axis_index("seq") % REQUESTS]
    score_scale = 1.0 / HEAD_DIM**0.5

    row = lax.broadcasted_iota(jnp.int32, (size, size), 0)
    column = lax.broadcasted_iota(jnp.int32, (size, size), 1)
    key_token = column // 8 * 2 + column % 2
    allowed = (row % 8 // 2 == column % 8 // 2) & (key_token < limit)

    def modulation(index, tile):
        value = rows_ref[index, :, tile * LANES : (tile + 1) * LANES]
        return jnp.broadcast_to(value[None], (devices, 8, LANES)).reshape(size, LANES)

    total = jnp.zeros((size, LANES), jnp.float32)
    for tile in range(tiles):
        q, k, v, h = [
            got_ref[
                :,
                table_rows + (kind * tiles + tile) * 8 : table_rows + (kind * tiles + tile) * 8 + 8,
                :,
            ].reshape(size, LANES)
            for kind in range(4)
        ]
        scores = jnp.where(allowed, nt_dot(q, k) * score_scale, -jnp.inf)
        peak = jnp.max(scores, axis=-1, keepdims=True)
        raised = jnp.exp(scores - peak)
        weights = raised / jnp.sum(raised, axis=-1, keepdims=True)
        attended = jnp.dot(
            weights.astype(jnp.bfloat16), v, preferred_element_type=jnp.float32
        ).astype(jnp.bfloat16)
        residual = h.astype(jnp.float32) + modulation(0, tile) * attended.astype(jnp.float32)
        residual_ref[tile] = residual
        total = total + residual
    mean = jnp.sum(group_sum(total), axis=-1, keepdims=True) * (1.0 / width)
    total = jnp.zeros((size, LANES), jnp.float32)
    for tile in range(tiles):
        centered = residual_ref[tile] - mean
        residual_ref[tile] = centered
        total = total + centered * centered
    variance = jnp.sum(group_sum(total), axis=-1, keepdims=True) * (1.0 / width)
    inverse = lax.rsqrt(variance + 1e-06)
    channels = head_ref.shape[0] // QUARTERS
    product = jnp.zeros((size, QUARTERS * channels), jnp.float32)
    for tile in range(tiles):
        normed = residual_ref[tile] * inverse * (1.0 + modulation(2, tile)) + modulation(1, tile)
        product = product + nt_dot(
            normed.astype(jnp.bfloat16), head_ref[:, tile * LANES : (tile + 1) * LANES]
        )
    row = lax.broadcasted_iota(jnp.int32, product.shape, 0)
    column = lax.broadcasted_iota(jnp.int32, product.shape, 1)
    product = jnp.where(row % 8 // 2 == column // channels, product, 0.0)
    product = group_sum(product[:, :LANES] + product[:, LANES:])
    product = product + pltpu.roll(product, channels, 1)
    bias = bias_ref[...]
    product = product + jnp.concatenate([bias, bias], axis=1)
    pick_ref[...] = product
    first_token = pick_ref[pl.ds(0, devices, stride=8), :]
    second_token = pick_ref[pl.ds(1, devices, stride=8), :]
    lane = lax.broadcasted_iota(jnp.int32, (devices, LANES), 1)
    stream_velocity = jnp.where(lane < channels, first_token, second_token)
    latent = jnp.concatenate([latent_ref[0], latent_ref[1]], axis=1)
    block = jnp.concatenate([stream_velocity, latent], axis=0)
    out_ref[...] = jnp.broadcast_to(block[None], out_ref.shape)


def finish_kernel(
    ids_ref,
    got_ref,
    guidance_ref,
    step_ref,
    gram_ref,
    near_ref,
    far_ref,
    velocity_ref,
    latent_ref,
    delta_ref,
    velocity_all,
    latent_all,
    product_ref,
    *,
    devices,
    columns,
    half_tiles,
):
    block = devices + REQUESTS
    request_row = lax.broadcasted_iota(jnp.int32, (REQUESTS, LANES), 0)
    guidance = jnp.zeros((REQUESTS, LANES), jnp.float32)
    position = jnp.zeros((REQUESTS, LANES), jnp.int32)
    for request in range(REQUESTS):
        guidance = jnp.where(request_row == request, guidance_ref[request], guidance)
        position = jnp.where(request_row == request, step_ref[request], position)
    sigma_now = noise_level(position.astype(jnp.float32))
    step = noise_level((position + 1).astype(jnp.float32)) - sigma_now
    lane = lax.broadcasted_iota(jnp.int32, (REQUESTS, LANES), 1)
    channels = LANES // 2
    pieces = []
    for source in range(devices):
        conditional = got_ref[pl.ds(source, REQUESTS, stride=block), :]
        unconditional = got_ref[pl.ds(REQUESTS * block + source, REQUESTS, stride=block), :]
        velocity = unconditional + guidance * (conditional - unconditional)
        first = source * block + devices
        latent_next = got_ref[first : first + REQUESTS, :] + step * velocity
        velocity_all[source] = velocity
        latent_all[source] = latent_next
        tail = jnp.where(lane < channels + 3, 1.0, 0.0)
        pieces.append(jnp.where(lane < channels, latent_next, tail))
        pieces.append(jnp.where(lane < channels, pltpu.roll(latent_next, channels, 1), tail))
    mine = lax.axis_index("seq")
    velocity = velocity_all[mine]
    latent_next = latent_all[mine]
    velocity_ref[0] = velocity[:, :channels]
    velocity_ref[1] = velocity[:, channels:]
    latent_ref[0] = latent_next[:, :channels]
    latent_ref[1] = latent_next[:, channels:]

    rounded = jnp.concatenate(pieces, axis=0).astype(jnp.bfloat16)
    rows = rounded.shape[0]
    exact = rounded.astype(jnp.float32)
    used = gram_ref.shape[0]
    image = jnp.dot(
        exact[:, :used],
        gram_ref[...],
        precision=lax.Precision.HIGHEST,
        preferred_element_type=jnp.float32,
    )
    spread = jnp.sum(image * exact[:, :used], axis=-1, keepdims=True)
    inverse = lax.rsqrt(spread * (1.0 / (HEADS * HEAD_DIM)) + 1e-06)

    request_of_row = lax.broadcasted_iota(jnp.int32, (rows, TABLE_ROWS), 0) % REQUESTS
    left = jnp.concatenate(
        [
            jnp.where(request_of_row == request, exact[:, :TABLE_ROWS], 0.0)
            for request in range(REQUESTS)
        ],
        axis=1,
    ).astype(jnp.bfloat16)
    half = half_tiles * LANES
    side = lax.axis_index("rep")

    def near(request, tile):
        return near_ref[ids_ref[request], tile * TABLE_ROWS : (tile + 1) * TABLE_ROWS, :]

    def far(request, tile):
        return far_ref[request, tile * TABLE_ROWS : (tile + 1) * TABLE_ROWS, :]

    for which, take in ((side, near), (1 - side, far)):
        right = jnp.concatenate(
            [
                jnp.concatenate([take(request, tile) for request in range(REQUESTS)], axis=0)
                for tile in range(half_tiles)
            ],
            axis=1,
        )
        product = jnp.dot(left, right, preferred_element_type=jnp.float32) * inverse
        product_ref[:, pl.ds(pl.multiple_of(which * half, LANES), half)] = product
    shape = delta_ref.shape
    offsets = sorted({columns * target % LANES for target in range(devices)})
    own = columns * mine % LANES
    for offset in offsets:

        @pl.when(own == offset)
        def _(offset=offset):
            kept = product_ref[:, offset : offset + columns]
            delta_ref[...] = kept.astype(jnp.bfloat16).reshape(shape)


def broadcast(value, axis, source):
    kept = jnp.where(lax.axis_index(axis) == source, value, 0).astype(value.dtype)
    return lax.psum(kept, axis)


def noise_level(position):
    fraction = 1.0 - position / STEPS
    return 5.0 * fraction / (1.0 + 4.0 * fraction)


def layer_normed(rows):
    row_mean = jnp.mean(rows, axis=-1, keepdims=True)
    centered = rows - row_mean
    row_var = jnp.mean(centered * centered, axis=-1, keepdims=True)
    return centered * lax.rsqrt(row_var + 1e-06)


def many_per_stream(
    queries,
    key_states,
    value_states,
    hidden,
    residual_gate,
    head_shift,
    head_scale,
    head_weight,
    head_bias,
    guidance,
    step_index,
    lengths,
    latent,
    embed_weight,
    embed_bias,
    adapter_ids,
    adapter_down,
    adapter_up,
):
    row_count, stream_count, feature_width = queries.shape
    axis_devices = lax.axis_size("seq")
    full_length = row_count * axis_devices
    item_count = stream_count * feature_width // HEAD_DIM
    local_items = item_count // axis_devices
    score_scale = 1.0 / HEAD_DIM**0.5

    def as_items(states):
        return states.reshape(row_count, item_count, HEAD_DIM)

    query_heads, key_heads, value_heads = (
        lax.all_to_all(as_items(queries), "seq", split_axis=1, concat_axis=0, tiled=True),
        lax.all_to_all(as_items(key_states), "seq", split_axis=1, concat_axis=0, tiled=True),
        lax.all_to_all(as_items(value_states), "seq", split_axis=1, concat_axis=0, tiled=True),
    )
    first_item = lax.axis_index("seq") * local_items
    item_request = (first_item + jnp.arange(local_items)) // HEADS % REQUESTS
    selector = (item_request[:, None] == jnp.arange(REQUESTS)[None, :]).astype(jnp.int32)
    key_limit = jnp.sum(selector * lengths[None, :], axis=1)

    def attend(operands):
        query_rows, key_rows, value_rows, key_bound = operands
        scores = (
            jnp.einsum("qd,kd->qk", query_rows, key_rows, preferred_element_type=jnp.float32)
            * score_scale
        )
        allowed = jnp.arange(full_length)[None, :] < key_bound
        scores = jnp.where(allowed, scores, -jnp.inf)
        weights = jax.nn.softmax(scores, axis=-1).astype(jnp.bfloat16)
        return jnp.dot(weights, value_rows, preferred_element_type=jnp.float32).astype(jnp.bfloat16)

    attended_items = lax.map(
        attend,
        (
            jnp.moveaxis(query_heads, 1, 0),
            jnp.moveaxis(key_heads, 1, 0),
            jnp.moveaxis(value_heads, 1, 0),
            key_limit,
        ),
    )
    returned = lax.all_to_all(
        jnp.moveaxis(attended_items, 0, 1), "seq", split_axis=0, concat_axis=1, tiled=True
    )
    attended = returned.reshape(row_count, stream_count, feature_width)
    residual = hidden.astype(jnp.float32) + residual_gate[None, :, :] * attended.astype(jnp.float32)
    normed = (layer_normed(residual) * (1.0 + head_scale[None]) + head_shift[None]).astype(
        jnp.bfloat16
    )
    stream_velocity = jnp.dot(
        normed.reshape(-1, feature_width), head_weight, preferred_element_type=jnp.float32
    )
    stream_velocity = stream_velocity.reshape(row_count, stream_count, -1) + head_bias
    conditional = stream_velocity[:, :REQUESTS]
    unconditional = stream_velocity[:, REQUESTS:]
    velocity = unconditional + guidance[None, :, None] * (conditional - unconditional)
    sigma_now = noise_level(step_index.astype(jnp.float32))
    sigma_next = noise_level((step_index + 1).astype(jnp.float32))
    latent_next = latent + (sigma_next - sigma_now)[None, :, None] * velocity
    latent_rounded = latent_next.astype(jnp.bfloat16)
    held_slots = adapter_down.shape[0]
    embedded = jnp.dot(
        latent_rounded.reshape(row_count * REQUESTS, -1),
        embed_weight,
        preferred_element_type=jnp.float32,
    )
    embedded = embedded.reshape(row_count, REQUESTS, feature_width) + embed_bias
    block_input = layer_normed(embedded).astype(jnp.bfloat16)
    up_parts = lax.all_to_all(adapter_up, "seq", split_axis=1, concat_axis=0, tiled=True)
    user_count = up_parts.shape[0]
    chooser = (adapter_ids[:, None] == jnp.arange(user_count)[None, :]).astype(jnp.bfloat16)
    up_used = jnp.einsum(
        "ru,uck->rck", chooser, up_parts, preferred_element_type=jnp.float32
    ).astype(jnp.bfloat16)
    down_list = []
    for request in range(REQUESTS):
        owner_device = adapter_ids[request] // held_slots
        owner_slot = adapter_ids[request] % held_slots
        own_down = lax.dynamic_index_in_dim(adapter_down, owner_slot, 0, keepdims=False)
        whole_down = broadcast(own_down, "seq", owner_device)
        down_list.append(whole_down)
    down_used = jnp.stack(down_list, axis=0)
    low_rank = jnp.einsum(
        "lrd,rdk->lrk", block_input, down_used, preferred_element_type=jnp.float32
    ).astype(jnp.bfloat16)
    low_rank_all = lax.all_gather(low_rank, "seq", axis=0, tiled=True)
    adapter_delta = jnp.einsum(
        "lrk,rck->lrc", low_rank_all, up_used, preferred_element_type=jnp.float32
    ).astype(jnp.bfloat16)
    return (velocity, latent_next, adapter_delta)


def whole(shape):
    return pl.BlockSpec(shape, lambda *_: (0,) * len(shape))


def one_stream_each(
    queries,
    key_states,
    value_states,
    hidden,
    residual_gate,
    head_shift,
    head_scale,
    head_weight,
    head_bias,
    guidance,
    step_index,
    lengths,
    latent,
    embed_weight,
    embed_bias,
    adapter_ids,
    adapter_down,
    adapter_up,
):
    devices = lax.axis_size("seq")
    row_count, stream_count, width = queries.shape
    columns = adapter_up.shape[1] // devices
    half_tiles = window_tiles(columns, devices) // 2
    table_rows = half_tiles * TABLE_ROWS
    send_rows = table_rows + 4 * (width // QUARTERS // LANES) * 8
    swap = [(0, 1), (1, 0)]
    other_ids = lax.ppermute(adapter_ids, "rep", swap)
    smem = pl.BlockSpec(memory_space=pltpu.SMEM)
    vmem = pl.BlockSpec(memory_space=pltpu.VMEM)
    anywhere = pl.BlockSpec(memory_space=pl.ANY)
    params = pltpu.CompilerParams(vmem_limit_bytes=VMEM_LIMIT)

    sources = (
        queries,
        key_states,
        value_states,
        hidden,
        embed_weight,
        embed_bias[None, :],
        adapter_down[0].T,
        adapter_up[0].T,
    )
    send, gram = pl.pallas_call(
        functools.partial(
            prepare_kernel, devices=devices, columns=columns, half_tiles=half_tiles
        ),
        out_shape=(
            jax.ShapeDtypeStruct((devices, send_rows, LANES), jnp.bfloat16),
            jax.ShapeDtypeStruct((80, 80), jnp.float32),
        ),
        in_specs=[anywhere] * len(sources),
        out_specs=(vmem, vmem),
        scratch_shapes=[pltpu.VMEM(source.shape, source.dtype) for source in sources]
        + [pltpu.SemaphoreType.DMA((len(sources),))],
        compiler_params=pltpu.CompilerParams(vmem_limit_bytes=PREPARE_VMEM_LIMIT),
        name="prepare",
    )(*sources)
    got = lax.all_to_all(send, "seq", split_axis=0, concat_axis=0, tiled=True)

    chosen = pl.pallas_call(
        choose_kernel,
        out_shape=jax.ShapeDtypeStruct((REQUESTS, table_rows, LANES), jnp.bfloat16),
        in_specs=[smem, anywhere],
        out_specs=anywhere,
        scratch_shapes=[pltpu.SemaphoreType.DMA((REQUESTS,))],
        compiler_params=params,
        name="choose",
    )(other_ids, got)
    far = lax.ppermute(chosen, "rep", swap)

    quarter = width // QUARTERS
    channels = head_weight.shape[1]
    rows, head = pl.pallas_call(
        modulate_kernel,
        out_shape=(
            jax.ShapeDtypeStruct((3, 8, quarter), jnp.float32),
            jax.ShapeDtypeStruct((QUARTERS * channels, quarter), head_weight.dtype),
        ),
        in_specs=[vmem] * 4,
        out_specs=(vmem, vmem),
        compiler_params=params,
        name="modulate",
    )(residual_gate, head_shift, head_scale, head_weight.T)
    payload_rows = devices + REQUESTS
    payload = pl.pallas_call(
        functools.partial(attend_kernel, table_rows=table_rows),
        out_shape=jax.ShapeDtypeStruct((devices, payload_rows, LANES), jnp.float32),
        in_specs=[smem] + [vmem] * 5,
        out_specs=vmem,
        scratch_shapes=[
            pltpu.VMEM((quarter // LANES, devices * 8, LANES), jnp.float32),
            pltpu.VMEM((devices * 8, LANES), jnp.float32),
        ],
        compiler_params=params,
        name="attend",
        cost_estimate=pl.CostEstimate(
            flops=10**9, bytes_accessed=4 * 10**6, transcendentals=2 * 10**5
        ),
    )(
        lengths,
        got,
        rows,
        head,
        head_bias[None, :],
        latent,
    )
    shared = lax.all_to_all(payload, "seq", split_axis=0, concat_axis=0, tiled=True)

    across = (REQUESTS, LANES)
    return pl.pallas_call(
        functools.partial(finish_kernel, devices=devices, columns=columns, half_tiles=half_tiles),
        out_shape=(
            jax.ShapeDtypeStruct(latent.shape, jnp.float32),
            jax.ShapeDtypeStruct(latent.shape, jnp.float32),
            jax.ShapeDtypeStruct((row_count * devices, REQUESTS, columns), jnp.bfloat16),
        ),
        in_specs=[smem, vmem, smem, smem] + [vmem] * 3,
        out_specs=(vmem, vmem, vmem),
        scratch_shapes=[
            pltpu.VMEM((devices,) + across, jnp.float32),
            pltpu.VMEM((devices,) + across, jnp.float32),
            pltpu.VMEM((row_count * devices * REQUESTS, 2 * half_tiles * LANES), jnp.float32),
        ],
        compiler_params=params,
        name="finish",
    )(
        adapter_ids,
        shared.reshape(devices * payload_rows, LANES),
        guidance,
        step_index,
        gram,
        got,
        far,
    )


def window_tiles(columns, devices):
    most = max(
        pl.cdiv(columns * (d + 1), LANES) - columns * d // LANES for d in range(devices)
    )
    return (most + 1) // 2 * 2


def shards(*operands):
    queries, held, table = operands[0], operands[16], operands[17]
    row_count, stream_count, width = queries.shape
    devices = lax.axis_size("seq")
    columns = table.shape[1] // devices
    fits = (
        stream_count == devices
        and row_count == 2
        and held.shape[0] == 1
        and held.shape[2] == LANES // 2
        and lax.axis_size("rep") == 2
        and width % (QUARTERS * LANES) == 0
        and all(
            columns * d // LANES + window_tiles(columns, devices) <= table.shape[1] // LANES
            for d in range(devices)
        )
    )
    return one_stream_each(*operands) if fits else many_per_stream(*operands)


def solution(mesh):
    placed = (
        P("seq", "rep", None),
        P("seq", "rep", None),
        P("seq", "rep", None),
        P("seq", "rep", None),
        P("rep", None),
        P("rep", None),
        P("rep", None),
        P(),
        P(),
        P("rep"),
        P("rep"),
        P("rep"),
        P("seq", "rep", None),
        P(),
        P(),
        P("rep"),
        P("seq", None, None),
        P("seq", None, None),
    )
    return jax.shard_map(
        shards,
        mesh=mesh,
        in_specs=placed,
        out_specs=(P("seq", "rep", None), P("seq", "rep", None), P(None, "rep", "seq")),
        check_vma=False,
    )
```

```python
import functools

import jax
import jax.numpy as jnp
from jax import lax
from jax.experimental import pallas as pl
from jax.experimental.pallas import tpu as pltpu
from jax.sharding import PartitionSpec as P

HEADS = 40
HEAD_DIM = 128
REQUESTS = 8
STEPS = 10
LANES = 128
QUARTERS = 4
TABLE_ROWS = 64
BIAS_ROWS = 8
VMEM_LIMIT = 20 << 20
PREPARE_VMEM_LIMIT = 56 << 20

NT = (((1,), (1,)), ((), ()))


def nt_dot(a, b):
    return lax.dot_general(a, b, NT, preferred_element_type=jnp.float32)


def prepare_kernel(*refs, devices, columns, half_tiles):
    sources, (sent_ref, gram_ref), held = refs[:8], refs[8:10], refs[10:18]
    send_ref, sems, out_sems = refs[18:]
    copies = [
        pltpu.make_async_copy(source, target, sems.at[index])
        for index, (source, target) in enumerate(zip(sources, held))
    ]
    for copy in copies:
        copy.start()
    q_ref, k_ref, v_ref, h_ref, embed_ref, bias_ref, down_ref, up_ref = held
    row_count, stream_count, width = q_ref.shape
    quarter = width // QUARTERS
    tiles = quarter // LANES
    table_rows = half_tiles * TABLE_ROWS + BIAS_ROWS
    size = stream_count * 8
    to = lax.broadcasted_iota(jnp.int32, (size, size), 0)
    at = lax.broadcasted_iota(jnp.int32, (size, size), 1)
    same = (to // 8 == at % stream_count) & (to % 8 == at // stream_count)
    permutation = jnp.where(same, 1.0, 0.0).astype(jnp.bfloat16)
    for kind, ref in enumerate((q_ref, k_ref, v_ref, h_ref)):
        copies[kind].wait()
        stacked = jnp.concatenate(
            [
                ref[token, :, part * quarter : (part + 1) * quarter]
                for part in range(QUARTERS)
                for token in range(row_count)
            ],
            axis=0,
        )
        moved = jnp.dot(permutation, stacked, preferred_element_type=jnp.float32)
        moved = moved.astype(jnp.bfloat16)
        for tile in range(tiles):
            first = table_rows + (kind * tiles + tile) * 8
            send_ref[:, first : first + 8, :] = moved[
                :, tile * LANES : (tile + 1) * LANES
            ].reshape(stream_count, 8, LANES)

    writes = [
        pltpu.make_async_copy(
            send_ref.at[:, table_rows:], sent_ref.at[:, table_rows:], out_sems.at[0]
        )
    ]
    writes[0].start()

    for copy in copies[4:7]:
        copy.wait()
    bias = bias_ref[...]
    high = bias.astype(jnp.bfloat16).astype(jnp.float32)
    middle = (bias - high).astype(jnp.bfloat16).astype(jnp.float32)
    low = bias - high - middle
    row = lax.broadcasted_iota(jnp.int32, (16, width), 0)
    extra = jnp.where(row == 0, high, jnp.where(row == 1, middle, jnp.where(row == 2, low, 0.0)))
    extra = jnp.where(row == 3, 1.0, extra).astype(jnp.bfloat16)
    rows = jnp.concatenate([embed_ref[...], extra], axis=0)
    raw = nt_dot(rows, down_ref[...])
    gram = nt_dot(rows, rows)
    ones_at = 67
    sums = gram[:, ones_at : ones_at + 1]
    centered = raw - sums * (1.0 / width) * raw[ones_at : ones_at + 1, :]
    gram_ref[...] = gram - sums * (1.0 / width) * gram[ones_at : ones_at + 1, :]
    bias_row = centered[64:65] + centered[65:66] + centered[66:67]
    tail = lax.broadcasted_iota(jnp.int32, (8, centered.shape[1]), 0)
    mixing = jnp.concatenate(
        [centered[:64], jnp.where(tail == 0, jnp.broadcast_to(bias_row, tail.shape), 0.0)], axis=0
    )
    mixing_high = mixing.astype(jnp.bfloat16)
    mixing_low = (mixing - mixing_high.astype(jnp.float32)).astype(jnp.bfloat16)
    mixing = jnp.concatenate([mixing_high, mixing_low], axis=1)

    half = half_tiles * LANES
    side = lax.axis_index("rep") * half
    copies[7].wait()
    row = lax.broadcasted_iota(jnp.int32, (BIAS_ROWS, LANES), 0)
    for target in range(devices):
        start = columns * target // LANES * LANES
        part = up_ref[:, pl.ds(pl.multiple_of(start + side, LANES), half)]
        table = jnp.dot(
            mixing, jnp.concatenate([part, part], axis=0), preferred_element_type=jnp.float32
        )
        biases = jnp.zeros((BIAS_ROWS, LANES), jnp.float32)
        for tile in range(half_tiles):
            piece = table[:, tile * LANES : (tile + 1) * LANES]
            send_ref[target, tile * TABLE_ROWS : (tile + 1) * TABLE_ROWS, :] = piece[
                :TABLE_ROWS
            ].astype(jnp.bfloat16)
            biases = jnp.where(
                row == tile,
                jnp.broadcast_to(piece[TABLE_ROWS : TABLE_ROWS + 1], biases.shape),
                biases,
            )
        send_ref[target, half_tiles * TABLE_ROWS : table_rows, :] = biases.astype(jnp.bfloat16)
        writes.append(
            pltpu.make_async_copy(
                send_ref.at[target, 0:table_rows],
                sent_ref.at[target, 0:table_rows],
                out_sems.at[1 + target],
            )
        )
        writes[-1].start()
    for write in writes:
        write.wait()


def choose_kernel(ids_ref, got_ref, out_ref, sems):
    count = out_ref.shape[1]
    copies = [
        pltpu.make_async_copy(
            got_ref.at[ids_ref[request], 0:count],
            out_ref.at[request],
            sems.at[request],
        )
        for request in range(REQUESTS)
    ]
    for copy in copies:
        copy.start()
    for copy in copies:
        copy.wait()


def group_sum(x):
    grouped = x.reshape(x.shape[0] // 8, 8, x.shape[1])
    grouped = grouped + pltpu.roll(grouped, 2, 1)
    grouped = grouped + pltpu.roll(grouped, 4, 1)
    return grouped.reshape(x.shape)


def modulate_kernel(gate_ref, shift_ref, scale_ref, weight_ref, rows_ref, head_ref):
    width = gate_ref.shape[1]
    quarter = width // QUARTERS
    mine = lax.axis_index("seq")
    part_of_row = lax.broadcasted_iota(jnp.int32, (8, quarter), 0) // 2
    for index, ref in enumerate((gate_ref, shift_ref, scale_ref)):
        block = ref[pl.ds(pl.multiple_of(mine // 8 * 8, 8), 8), :]
        row = pltpu.roll(block, (8 - mine % 8) % 8, 0)[0:1]
        value = jnp.zeros((8, quarter), jnp.float32)
        for part in range(QUARTERS):
            piece = row[:, part * quarter : (part + 1) * quarter]
            value = jnp.where(part_of_row == part, jnp.broadcast_to(piece, value.shape), value)
        rows_ref[index] = value
    channels = weight_ref.shape[0]
    for part in range(QUARTERS):
        head_ref[part * channels : (part + 1) * channels, :] = weight_ref[
            :, part * quarter : (part + 1) * quarter
        ]


def attend_kernel(
    lengths_ref,
    got_ref,
    rows_ref,
    head_ref,
    bias_ref,
    latent_ref,
    out_ref,
    residual_ref,
    pick_ref,
    *,
    table_rows,
):
    devices = got_ref.shape[0]
    quarter = rows_ref.shape[2]
    width = quarter * QUARTERS
    tiles = quarter // LANES
    size = devices * 8
    limit = lengths_ref[lax.axis_index("seq") % REQUESTS]
    score_scale = 1.0 / HEAD_DIM**0.5

    row = lax.broadcasted_iota(jnp.int32, (size, size), 0)
    column = lax.broadcasted_iota(jnp.int32, (size, size), 1)
    key_token = column // 8 * 2 + column % 2
    allowed = (row % 8 // 2 == column % 8 // 2) & (key_token < limit)

    def modulation(index, tile):
        value = rows_ref[index, :, tile * LANES : (tile + 1) * LANES]
        return jnp.broadcast_to(value[None], (devices, 8, LANES)).reshape(size, LANES)

    total = jnp.zeros((size, LANES), jnp.float32)
    for tile in range(tiles):
        q, k, v, h = [
            got_ref[
                :,
                table_rows + (kind * tiles + tile) * 8 : table_rows + (kind * tiles + tile) * 8 + 8,
                :,
            ].reshape(size, LANES)
            for kind in range(4)
        ]
        scores = jnp.where(allowed, nt_dot(q, k) * score_scale, -jnp.inf)
        peak = jnp.max(scores, axis=-1, keepdims=True)
        raised = jnp.exp(scores - peak)
        weights = raised / jnp.sum(raised, axis=-1, keepdims=True)
        attended = jnp.dot(
            weights.astype(jnp.bfloat16), v, preferred_element_type=jnp.float32
        ).astype(jnp.bfloat16)
        residual = h.astype(jnp.float32) + modulation(0, tile) * attended.astype(jnp.float32)
        residual_ref[tile] = residual
        total = total + residual
    mean = jnp.sum(group_sum(total), axis=-1, keepdims=True) * (1.0 / width)
    total = jnp.zeros((size, LANES), jnp.float32)
    for tile in range(tiles):
        centered = residual_ref[tile] - mean
        residual_ref[tile] = centered
        total = total + centered * centered
    variance = jnp.sum(group_sum(total), axis=-1, keepdims=True) * (1.0 / width)
    inverse = lax.rsqrt(variance + 1e-06)
    channels = head_ref.shape[0] // QUARTERS
    product = jnp.zeros((size, QUARTERS * channels), jnp.float32)
    for tile in range(tiles):
        normed = residual_ref[tile] * inverse * (1.0 + modulation(2, tile)) + modulation(1, tile)
        product = product + nt_dot(
            normed.astype(jnp.bfloat16), head_ref[:, tile * LANES : (tile + 1) * LANES]
        )
    row = lax.broadcasted_iota(jnp.int32, product.shape, 0)
    column = lax.broadcasted_iota(jnp.int32, product.shape, 1)
    product = jnp.where(row % 8 // 2 == column // channels, product, 0.0)
    product = group_sum(product[:, :LANES] + product[:, LANES:])
    product = product + pltpu.roll(product, channels, 1)
    bias = bias_ref[...]
    product = product + jnp.concatenate([bias, bias], axis=1)
    pick_ref[...] = product
    first_token = pick_ref[pl.ds(0, devices, stride=8), :]
    second_token = pick_ref[pl.ds(1, devices, stride=8), :]
    lane = lax.broadcasted_iota(jnp.int32, (devices, LANES), 1)
    stream_velocity = jnp.where(lane < channels, first_token, second_token)
    latent = jnp.concatenate([latent_ref[0], latent_ref[1]], axis=1)
    block = jnp.concatenate([stream_velocity, latent], axis=0)
    out_ref[...] = jnp.broadcast_to(block[None], out_ref.shape)


def finish_kernel(
    ids_ref,
    got_ref,
    guidance_ref,
    step_ref,
    gram_ref,
    near_ref,
    far_ref,
    velocity_ref,
    latent_ref,
    delta_ref,
    velocity_all,
    latent_all,
    product_ref,
    *,
    devices,
    columns,
    half_tiles,
):
    block = devices + REQUESTS
    request_row = lax.broadcasted_iota(jnp.int32, (REQUESTS, LANES), 0)
    guidance = jnp.zeros((REQUESTS, LANES), jnp.float32)
    position = jnp.zeros((REQUESTS, LANES), jnp.int32)
    for request in range(REQUESTS):
        guidance = jnp.where(request_row == request, guidance_ref[request], guidance)
        position = jnp.where(request_row == request, step_ref[request], position)
    sigma_now = noise_level(position.astype(jnp.float32))
    step = noise_level((position + 1).astype(jnp.float32)) - sigma_now
    lane = lax.broadcasted_iota(jnp.int32, (REQUESTS, LANES), 1)
    channels = LANES // 2
    pieces = []
    for source in range(devices):
        conditional = got_ref[pl.ds(source, REQUESTS, stride=block), :]
        unconditional = got_ref[pl.ds(REQUESTS * block + source, REQUESTS, stride=block), :]
        velocity = unconditional + guidance * (conditional - unconditional)
        first = source * block + devices
        latent_next = got_ref[first : first + REQUESTS, :] + step * velocity
        velocity_all[source] = velocity
        latent_all[source] = latent_next
        tail = jnp.where(lane < channels + 3, 1.0, 0.0)
        pieces.append(jnp.where(lane < channels, latent_next, tail))
        pieces.append(jnp.where(lane < channels, pltpu.roll(latent_next, channels, 1), tail))
    mine = lax.axis_index("seq")
    velocity = velocity_all[mine]
    latent_next = latent_all[mine]
    velocity_ref[0] = velocity[:, :channels]
    velocity_ref[1] = velocity[:, channels:]
    latent_ref[0] = latent_next[:, :channels]
    latent_ref[1] = latent_next[:, channels:]

    rounded = jnp.concatenate(pieces, axis=0).astype(jnp.bfloat16)
    rows = rounded.shape[0]
    exact = rounded.astype(jnp.float32)
    used = gram_ref.shape[0]
    image = jnp.dot(
        exact[:, :used],
        gram_ref[...],
        precision=lax.Precision.HIGHEST,
        preferred_element_type=jnp.float32,
    )
    spread = jnp.sum(image * exact[:, :used], axis=-1, keepdims=True)
    inverse = lax.rsqrt(spread * (1.0 / (HEADS * HEAD_DIM)) + 1e-06)

    request_of_row = lax.broadcasted_iota(jnp.int32, (rows, TABLE_ROWS), 0) % REQUESTS
    left = jnp.concatenate(
        [
            jnp.where(request_of_row == request, exact[:, :TABLE_ROWS], 0.0)
            for request in range(REQUESTS)
        ],
        axis=1,
    ).astype(jnp.bfloat16)
    half = half_tiles * LANES
    side = lax.axis_index("rep")

    def near(request, first, last):
        return near_ref[ids_ref[request], first:last, :]

    def far(request, first, last):
        return far_ref[request, first:last, :]

    bias_row = lax.broadcasted_iota(jnp.int32, (REQUESTS, LANES), 0)
    bias_at = half_tiles * TABLE_ROWS
    for which, take in ((side, near), (1 - side, far)):
        right = jnp.concatenate(
            [
                jnp.concatenate(
                    [
                        take(request, tile * TABLE_ROWS, (tile + 1) * TABLE_ROWS)
                        for request in range(REQUESTS)
                    ],
                    axis=0,
                )
                for tile in range(half_tiles)
            ],
            axis=1,
        )
        biases = [jnp.zeros((REQUESTS, LANES), jnp.float32)] * half_tiles
        for request in range(REQUESTS):
            block = take(request, bias_at, bias_at + BIAS_ROWS).astype(jnp.float32)
            biases = [
                jnp.where(bias_row == request, jnp.broadcast_to(block[t : t + 1], bias.shape), bias)
                for t, bias in enumerate(biases)
            ]
        bias = jnp.concatenate(biases, axis=1)
        product = jnp.dot(left, right, preferred_element_type=jnp.float32)
        product = product.reshape(rows // REQUESTS, REQUESTS, half) + bias[None]
        product_ref[:, pl.ds(pl.multiple_of(which * half, LANES), half)] = (
            product.reshape(rows, half) * inverse
        )
    shape = delta_ref.shape
    offsets = sorted({columns * target % LANES for target in range(devices)})
    own = columns * mine % LANES
    for offset in offsets:

        @pl.when(own == offset)
        def _(offset=offset):
            kept = product_ref[:, offset : offset + columns]
            delta_ref[...] = kept.astype(jnp.bfloat16).reshape(shape)


def broadcast(value, axis, source):
    kept = jnp.where(lax.axis_index(axis) == source, value, 0).astype(value.dtype)
    return lax.psum(kept, axis)


def noise_level(position):
    fraction = 1.0 - position / STEPS
    return 5.0 * fraction / (1.0 + 4.0 * fraction)


def layer_normed(rows):
    row_mean = jnp.mean(rows, axis=-1, keepdims=True)
    centered = rows - row_mean
    row_var = jnp.mean(centered * centered, axis=-1, keepdims=True)
    return centered * lax.rsqrt(row_var + 1e-06)


def many_per_stream(
    queries,
    key_states,
    value_states,
    hidden,
    residual_gate,
    head_shift,
    head_scale,
    head_weight,
    head_bias,
    guidance,
    step_index,
    lengths,
    latent,
    embed_weight,
    embed_bias,
    adapter_ids,
    adapter_down,
    adapter_up,
):
    row_count, stream_count, feature_width = queries.shape
    axis_devices = lax.axis_size("seq")
    full_length = row_count * axis_devices
    item_count = stream_count * feature_width // HEAD_DIM
    local_items = item_count // axis_devices
    score_scale = 1.0 / HEAD_DIM**0.5

    def as_items(states):
        return states.reshape(row_count, item_count, HEAD_DIM)

    query_heads, key_heads, value_heads = (
        lax.all_to_all(as_items(queries), "seq", split_axis=1, concat_axis=0, tiled=True),
        lax.all_to_all(as_items(key_states), "seq", split_axis=1, concat_axis=0, tiled=True),
        lax.all_to_all(as_items(value_states), "seq", split_axis=1, concat_axis=0, tiled=True),
    )
    first_item = lax.axis_index("seq") * local_items
    item_request = (first_item + jnp.arange(local_items)) // HEADS % REQUESTS
    selector = (item_request[:, None] == jnp.arange(REQUESTS)[None, :]).astype(jnp.int32)
    key_limit = jnp.sum(selector * lengths[None, :], axis=1)

    def attend(operands):
        query_rows, key_rows, value_rows, key_bound = operands
        scores = (
            jnp.einsum("qd,kd->qk", query_rows, key_rows, preferred_element_type=jnp.float32)
            * score_scale
        )
        allowed = jnp.arange(full_length)[None, :] < key_bound
        scores = jnp.where(allowed, scores, -jnp.inf)
        weights = jax.nn.softmax(scores, axis=-1).astype(jnp.bfloat16)
        return jnp.dot(weights, value_rows, preferred_element_type=jnp.float32).astype(jnp.bfloat16)

    attended_items = lax.map(
        attend,
        (
            jnp.moveaxis(query_heads, 1, 0),
            jnp.moveaxis(key_heads, 1, 0),
            jnp.moveaxis(value_heads, 1, 0),
            key_limit,
        ),
    )
    returned = lax.all_to_all(
        jnp.moveaxis(attended_items, 0, 1), "seq", split_axis=0, concat_axis=1, tiled=True
    )
    attended = returned.reshape(row_count, stream_count, feature_width)
    residual = hidden.astype(jnp.float32) + residual_gate[None, :, :] * attended.astype(jnp.float32)
    normed = (layer_normed(residual) * (1.0 + head_scale[None]) + head_shift[None]).astype(
        jnp.bfloat16
    )
    stream_velocity = jnp.dot(
        normed.reshape(-1, feature_width), head_weight, preferred_element_type=jnp.float32
    )
    stream_velocity = stream_velocity.reshape(row_count, stream_count, -1) + head_bias
    conditional = stream_velocity[:, :REQUESTS]
    unconditional = stream_velocity[:, REQUESTS:]
    velocity = unconditional + guidance[None, :, None] * (conditional - unconditional)
    sigma_now = noise_level(step_index.astype(jnp.float32))
    sigma_next = noise_level((step_index + 1).astype(jnp.float32))
    latent_next = latent + (sigma_next - sigma_now)[None, :, None] * velocity
    latent_rounded = latent_next.astype(jnp.bfloat16)
    held_slots = adapter_down.shape[0]
    embedded = jnp.dot(
        latent_rounded.reshape(row_count * REQUESTS, -1),
        embed_weight,
        preferred_element_type=jnp.float32,
    )
    embedded = embedded.reshape(row_count, REQUESTS, feature_width) + embed_bias
    block_input = layer_normed(embedded).astype(jnp.bfloat16)
    up_parts = lax.all_to_all(adapter_up, "seq", split_axis=1, concat_axis=0, tiled=True)
    user_count = up_parts.shape[0]
    chooser = (adapter_ids[:, None] == jnp.arange(user_count)[None, :]).astype(jnp.bfloat16)
    up_used = jnp.einsum(
        "ru,uck->rck", chooser, up_parts, preferred_element_type=jnp.float32
    ).astype(jnp.bfloat16)
    down_list = []
    for request in range(REQUESTS):
        owner_device = adapter_ids[request] // held_slots
        owner_slot = adapter_ids[request] % held_slots
        own_down = lax.dynamic_index_in_dim(adapter_down, owner_slot, 0, keepdims=False)
        whole_down = broadcast(own_down, "seq", owner_device)
        down_list.append(whole_down)
    down_used = jnp.stack(down_list, axis=0)
    low_rank = jnp.einsum(
        "lrd,rdk->lrk", block_input, down_used, preferred_element_type=jnp.float32
    ).astype(jnp.bfloat16)
    low_rank_all = lax.all_gather(low_rank, "seq", axis=0, tiled=True)
    adapter_delta = jnp.einsum(
        "lrk,rck->lrc", low_rank_all, up_used, preferred_element_type=jnp.float32
    ).astype(jnp.bfloat16)
    return (velocity, latent_next, adapter_delta)


def whole(shape):
    return pl.BlockSpec(shape, lambda *_: (0,) * len(shape))


def one_stream_each(
    queries,
    key_states,
    value_states,
    hidden,
    residual_gate,
    head_shift,
    head_scale,
    head_weight,
    head_bias,
    guidance,
    step_index,
    lengths,
    latent,
    embed_weight,
    embed_bias,
    adapter_ids,
    adapter_down,
    adapter_up,
):
    devices = lax.axis_size("seq")
    row_count, stream_count, width = queries.shape
    columns = adapter_up.shape[1] // devices
    half_tiles = window_tiles(columns, devices) // 2
    table_rows = half_tiles * TABLE_ROWS + BIAS_ROWS
    send_rows = table_rows + 4 * (width // QUARTERS // LANES) * 8
    swap = [(0, 1), (1, 0)]
    other_ids = lax.ppermute(adapter_ids, "rep", swap)
    smem = pl.BlockSpec(memory_space=pltpu.SMEM)
    vmem = pl.BlockSpec(memory_space=pltpu.VMEM)
    anywhere = pl.BlockSpec(memory_space=pl.ANY)
    params = pltpu.CompilerParams(vmem_limit_bytes=VMEM_LIMIT)

    sources = (
        queries,
        key_states,
        value_states,
        hidden,
        embed_weight,
        embed_bias[None, :],
        adapter_down[0].T,
        adapter_up[0].T,
    )
    send, gram = pl.pallas_call(
        functools.partial(
            prepare_kernel, devices=devices, columns=columns, half_tiles=half_tiles
        ),
        out_shape=(
            jax.ShapeDtypeStruct((devices, send_rows, LANES), jnp.bfloat16),
            jax.ShapeDtypeStruct((80, 80), jnp.float32),
        ),
        in_specs=[anywhere] * len(sources),
        out_specs=(anywhere, vmem),
        scratch_shapes=[pltpu.VMEM(source.shape, source.dtype) for source in sources]
        + [
            pltpu.VMEM((devices, send_rows, LANES), jnp.bfloat16),
            pltpu.SemaphoreType.DMA((len(sources),)),
            pltpu.SemaphoreType.DMA((1 + devices,)),
        ],
        compiler_params=pltpu.CompilerParams(vmem_limit_bytes=PREPARE_VMEM_LIMIT),
        name="prepare",
    )(*sources)
    got = lax.all_to_all(send, "seq", split_axis=0, concat_axis=0, tiled=True)

    chosen = pl.pallas_call(
        choose_kernel,
        out_shape=jax.ShapeDtypeStruct((REQUESTS, table_rows, LANES), jnp.bfloat16),
        in_specs=[smem, anywhere],
        out_specs=anywhere,
        scratch_shapes=[pltpu.SemaphoreType.DMA((REQUESTS,))],
        compiler_params=params,
        name="choose",
    )(other_ids, got)
    far = lax.ppermute(chosen, "rep", swap)

    quarter = width // QUARTERS
    channels = head_weight.shape[1]
    rows, head = pl.pallas_call(
        modulate_kernel,
        out_shape=(
            jax.ShapeDtypeStruct((3, 8, quarter), jnp.float32),
            jax.ShapeDtypeStruct((QUARTERS * channels, quarter), head_weight.dtype),
        ),
        in_specs=[vmem] * 4,
        out_specs=(vmem, vmem),
        compiler_params=params,
        name="modulate",
    )(residual_gate, head_shift, head_scale, head_weight.T)
    payload_rows = devices + REQUESTS
    payload = pl.pallas_call(
        functools.partial(attend_kernel, table_rows=table_rows),
        out_shape=jax.ShapeDtypeStruct((devices, payload_rows, LANES), jnp.float32),
        in_specs=[smem] + [vmem] * 5,
        out_specs=vmem,
        scratch_shapes=[
            pltpu.VMEM((quarter // LANES, devices * 8, LANES), jnp.float32),
            pltpu.VMEM((devices * 8, LANES), jnp.float32),
        ],
        compiler_params=params,
        name="attend",
        cost_estimate=pl.CostEstimate(
            flops=10**9, bytes_accessed=4 * 10**6, transcendentals=2 * 10**5
        ),
    )(
        lengths,
        got,
        rows,
        head,
        head_bias[None, :],
        latent,
    )
    shared = lax.all_to_all(payload, "seq", split_axis=0, concat_axis=0, tiled=True)

    across = (REQUESTS, LANES)
    return pl.pallas_call(
        functools.partial(finish_kernel, devices=devices, columns=columns, half_tiles=half_tiles),
        out_shape=(
            jax.ShapeDtypeStruct(latent.shape, jnp.float32),
            jax.ShapeDtypeStruct(latent.shape, jnp.float32),
            jax.ShapeDtypeStruct((row_count * devices, REQUESTS, columns), jnp.bfloat16),
        ),
        in_specs=[smem, vmem, smem, smem] + [vmem] * 3,
        out_specs=(vmem, vmem, vmem),
        scratch_shapes=[
            pltpu.VMEM((devices,) + across, jnp.float32),
            pltpu.VMEM((devices,) + across, jnp.float32),
            pltpu.VMEM((row_count * devices * REQUESTS, 2 * half_tiles * LANES), jnp.float32),
        ],
        compiler_params=params,
        name="finish",
    )(
        adapter_ids,
        shared.reshape(devices * payload_rows, LANES),
        guidance,
        step_index,
        gram,
        got,
        far,
    )


def window_tiles(columns, devices):
    most = max(
        pl.cdiv(columns * (d + 1), LANES) - columns * d // LANES for d in range(devices)
    )
    return (most + 1) // 2 * 2


def shards(*operands):
    queries, held, table = operands[0], operands[16], operands[17]
    row_count, stream_count, width = queries.shape
    devices = lax.axis_size("seq")
    columns = table.shape[1] // devices
    fits = (
        stream_count == devices
        and row_count == 2
        and held.shape[0] == 1
        and held.shape[2] == LANES // 2
        and lax.axis_size("rep") == 2
        and width % (QUARTERS * LANES) == 0
        and all(
            columns * d // LANES + window_tiles(columns, devices) <= table.shape[1] // LANES
            for d in range(devices)
        )
    )
    return one_stream_each(*operands) if fits else many_per_stream(*operands)


def solution(mesh):
    placed = (
        P("seq", "rep", None),
        P("seq", "rep", None),
        P("seq", "rep", None),
        P("seq", "rep", None),
        P("rep", None),
        P("rep", None),
        P("rep", None),
        P(),
        P(),
        P("rep"),
        P("rep"),
        P("rep"),
        P("seq", "rep", None),
        P(),
        P(),
        P("rep"),
        P("seq", None, None),
        P("seq", None, None),
    )
    return jax.shard_map(
        shards,
        mesh=mesh,
        in_specs=placed,
        out_specs=(P("seq", "rep", None), P("seq", "rep", None), P(None, "rep", "seq")),
        check_vma=False,
    )
```

```python
import functools

import jax
import jax.numpy as jnp
from jax import lax
from jax.experimental import pallas as pl
from jax.experimental.pallas import tpu as pltpu
from jax.sharding import PartitionSpec as P

HEADS = 40
HEAD_DIM = 128
REQUESTS = 8
STEPS = 10
LANES = 128
QUARTERS = 4
TABLE_ROWS = 64
BIAS_ROWS = 8
VMEM_LIMIT = 20 << 20
PREPARE_VMEM_LIMIT = 56 << 20

NT = (((1,), (1,)), ((), ()))


def nt_dot(a, b):
    return lax.dot_general(a, b, NT, preferred_element_type=jnp.float32)


def prepare_kernel(*refs, devices, columns, half_tiles):
    sources, (sent_ref, gram_ref), held = refs[:8], refs[8:10], refs[10:18]
    send_ref, sems, out_sems = refs[18:]
    copies = [
        pltpu.make_async_copy(source, target, sems.at[index])
        for index, (source, target) in enumerate(zip(sources, held))
    ]
    for copy in copies:
        copy.start()
    q_ref, k_ref, v_ref, h_ref, embed_ref, bias_ref, down_ref, up_ref = held
    row_count, stream_count, width = q_ref.shape
    quarter = width // QUARTERS
    tiles = quarter // LANES
    table_rows = half_tiles * TABLE_ROWS + BIAS_ROWS
    size = stream_count * 8
    to = lax.broadcasted_iota(jnp.int32, (size, size), 0)
    at = lax.broadcasted_iota(jnp.int32, (size, size), 1)
    same = (to // 8 == at % stream_count) & (to % 8 == at // stream_count)
    permutation = jnp.where(same, 1.0, 0.0).astype(jnp.bfloat16)
    for kind, ref in enumerate((q_ref, k_ref, v_ref, h_ref)):
        copies[kind].wait()
        stacked = jnp.concatenate(
            [
                ref[token, :, part * quarter : (part + 1) * quarter]
                for part in range(QUARTERS)
                for token in range(row_count)
            ],
            axis=0,
        )
        moved = jnp.dot(permutation, stacked, preferred_element_type=jnp.float32)
        moved = moved.astype(jnp.bfloat16)
        for tile in range(tiles):
            first = table_rows + (kind * tiles + tile) * 8
            send_ref[:, first : first + 8, :] = moved[
                :, tile * LANES : (tile + 1) * LANES
            ].reshape(stream_count, 8, LANES)

    writes = [
        pltpu.make_async_copy(
            send_ref.at[:, table_rows:], sent_ref.at[:, table_rows:], out_sems.at[0]
        )
    ]
    writes[0].start()

    for copy in copies[4:7]:
        copy.wait()
    bias = bias_ref[...]
    high = bias.astype(jnp.bfloat16).astype(jnp.float32)
    middle = (bias - high).astype(jnp.bfloat16).astype(jnp.float32)
    low = bias - high - middle
    row = lax.broadcasted_iota(jnp.int32, (16, width), 0)
    extra = jnp.where(row == 0, high, jnp.where(row == 1, middle, jnp.where(row == 2, low, 0.0)))
    extra = jnp.where(row == 3, 1.0, extra).astype(jnp.bfloat16)
    rows = jnp.concatenate([embed_ref[...], extra], axis=0)
    raw = nt_dot(rows, down_ref[...])
    gram = nt_dot(rows, rows)
    ones_at = 67
    sums = gram[:, ones_at : ones_at + 1]
    centered = raw - sums * (1.0 / width) * raw[ones_at : ones_at + 1, :]
    gram_ref[...] = gram - sums * (1.0 / width) * gram[ones_at : ones_at + 1, :]
    bias_row = centered[64:65] + centered[65:66] + centered[66:67]
    tail = lax.broadcasted_iota(jnp.int32, (8, centered.shape[1]), 0)
    mixing = jnp.concatenate(
        [centered[:64], jnp.where(tail == 0, jnp.broadcast_to(bias_row, tail.shape), 0.0)], axis=0
    )
    mixing_high = mixing.astype(jnp.bfloat16)
    mixing_low = (mixing - mixing_high.astype(jnp.float32)).astype(jnp.bfloat16)
    mixing = jnp.concatenate([mixing_high, mixing_low], axis=1)

    half = half_tiles * LANES
    side = lax.axis_index("rep") * half
    copies[7].wait()
    row = lax.broadcasted_iota(jnp.int32, (BIAS_ROWS, LANES), 0)
    for target in range(devices):
        start = columns * target // LANES * LANES
        part = up_ref[:, pl.ds(pl.multiple_of(start + side, LANES), half)]
        table = jnp.dot(
            mixing, jnp.concatenate([part, part], axis=0), preferred_element_type=jnp.float32
        )
        biases = jnp.zeros((BIAS_ROWS, LANES), jnp.float32)
        for tile in range(half_tiles):
            piece = table[:, tile * LANES : (tile + 1) * LANES]
            send_ref[target, tile * TABLE_ROWS : (tile + 1) * TABLE_ROWS, :] = piece[
                :TABLE_ROWS
            ].astype(jnp.bfloat16)
            biases = jnp.where(
                row == tile,
                jnp.broadcast_to(piece[TABLE_ROWS : TABLE_ROWS + 1], biases.shape),
                biases,
            )
        send_ref[target, half_tiles * TABLE_ROWS : table_rows, :] = biases.astype(jnp.bfloat16)
        writes.append(
            pltpu.make_async_copy(
                send_ref.at[target, 0:table_rows],
                sent_ref.at[target, 0:table_rows],
                out_sems.at[1 + target],
            )
        )
        writes[-1].start()
    for write in writes:
        write.wait()


def choose_kernel(ids_ref, got_ref, out_ref):
    count = out_ref.shape[1]
    for request in range(REQUESTS):
        out_ref[request] = got_ref[ids_ref[request], 0:count, :]


def group_sum(x):
    grouped = x.reshape(x.shape[0] // 8, 8, x.shape[1])
    grouped = grouped + pltpu.roll(grouped, 2, 1)
    grouped = grouped + pltpu.roll(grouped, 4, 1)
    return grouped.reshape(x.shape)


def modulate_kernel(gate_ref, shift_ref, scale_ref, weight_ref, rows_ref, head_ref):
    width = gate_ref.shape[1]
    quarter = width // QUARTERS
    mine = lax.axis_index("seq")
    part_of_row = lax.broadcasted_iota(jnp.int32, (8, quarter), 0) // 2
    for index, ref in enumerate((gate_ref, shift_ref, scale_ref)):
        block = ref[pl.ds(pl.multiple_of(mine // 8 * 8, 8), 8), :]
        row = pltpu.roll(block, (8 - mine % 8) % 8, 0)[0:1]
        value = jnp.zeros((8, quarter), jnp.float32)
        for part in range(QUARTERS):
            piece = row[:, part * quarter : (part + 1) * quarter]
            value = jnp.where(part_of_row == part, jnp.broadcast_to(piece, value.shape), value)
        rows_ref[index] = value
    channels = weight_ref.shape[0]
    for part in range(QUARTERS):
        head_ref[part * channels : (part + 1) * channels, :] = weight_ref[
            :, part * quarter : (part + 1) * quarter
        ]


def attend_kernel(
    lengths_ref,
    got_ref,
    rows_ref,
    head_ref,
    bias_ref,
    latent_ref,
    out_ref,
    residual_ref,
    pick_ref,
    *,
    table_rows,
):
    devices = got_ref.shape[0]
    quarter = rows_ref.shape[2]
    width = quarter * QUARTERS
    tiles = quarter // LANES
    size = devices * 8
    limit = lengths_ref[lax.axis_index("seq") % REQUESTS]
    score_scale = 1.0 / HEAD_DIM**0.5

    row = lax.broadcasted_iota(jnp.int32, (size, size), 0)
    column = lax.broadcasted_iota(jnp.int32, (size, size), 1)
    key_token = column // 8 * 2 + column % 2
    allowed = (row % 8 // 2 == column % 8 // 2) & (key_token < limit)

    def modulation(index, tile):
        value = rows_ref[index, :, tile * LANES : (tile + 1) * LANES]
        return jnp.broadcast_to(value[None], (devices, 8, LANES)).reshape(size, LANES)

    total = jnp.zeros((size, LANES), jnp.float32)
    for tile in range(tiles):
        q, k, v, h = [
            got_ref[
                :,
                table_rows + (kind * tiles + tile) * 8 : table_rows + (kind * tiles + tile) * 8 + 8,
                :,
            ].reshape(size, LANES)
            for kind in range(4)
        ]
        scores = jnp.where(allowed, nt_dot(q, k) * score_scale, -jnp.inf)
        peak = jnp.max(scores, axis=-1, keepdims=True)
        raised = jnp.exp(scores - peak)
        weights = raised / jnp.sum(raised, axis=-1, keepdims=True)
        attended = jnp.dot(
            weights.astype(jnp.bfloat16), v, preferred_element_type=jnp.float32
        ).astype(jnp.bfloat16)
        residual = h.astype(jnp.float32) + modulation(0, tile) * attended.astype(jnp.float32)
        residual_ref[tile] = residual
        total = total + residual
    mean = jnp.sum(group_sum(total), axis=-1, keepdims=True) * (1.0 / width)
    total = jnp.zeros((size, LANES), jnp.float32)
    for tile in range(tiles):
        centered = residual_ref[tile] - mean
        residual_ref[tile] = centered
        total = total + centered * centered
    variance = jnp.sum(group_sum(total), axis=-1, keepdims=True) * (1.0 / width)
    inverse = lax.rsqrt(variance + 1e-06)
    channels = head_ref.shape[0] // QUARTERS
    product = jnp.zeros((size, QUARTERS * channels), jnp.float32)
    for tile in range(tiles):
        normed = residual_ref[tile] * inverse * (1.0 + modulation(2, tile)) + modulation(1, tile)
        product = product + nt_dot(
            normed.astype(jnp.bfloat16), head_ref[:, tile * LANES : (tile + 1) * LANES]
        )
    row = lax.broadcasted_iota(jnp.int32, product.shape, 0)
    column = lax.broadcasted_iota(jnp.int32, product.shape, 1)
    product = jnp.where(row % 8 // 2 == column // channels, product, 0.0)
    product = group_sum(product[:, :LANES] + product[:, LANES:])
    product = product + pltpu.roll(product, channels, 1)
    bias = bias_ref[...]
    product = product + jnp.concatenate([bias, bias], axis=1)
    pick_ref[...] = product
    first_token = pick_ref[pl.ds(0, devices, stride=8), :]
    second_token = pick_ref[pl.ds(1, devices, stride=8), :]
    lane = lax.broadcasted_iota(jnp.int32, (devices, LANES), 1)
    stream_velocity = jnp.where(lane < channels, first_token, second_token)
    latent = jnp.concatenate([latent_ref[0], latent_ref[1]], axis=1)
    block = jnp.concatenate([stream_velocity, latent], axis=0)
    out_ref[...] = jnp.broadcast_to(block[None], out_ref.shape)


def finish_kernel(
    ids_ref,
    got_ref,
    guidance_ref,
    step_ref,
    gram_ref,
    near_ref,
    far_ref,
    velocity_ref,
    latent_ref,
    delta_ref,
    velocity_all,
    latent_all,
    product_ref,
    *,
    devices,
    columns,
    half_tiles,
):
    block = devices + REQUESTS
    request_row = lax.broadcasted_iota(jnp.int32, (REQUESTS, LANES), 0)
    guidance = jnp.zeros((REQUESTS, LANES), jnp.float32)
    position = jnp.zeros((REQUESTS, LANES), jnp.int32)
    for request in range(REQUESTS):
        guidance = jnp.where(request_row == request, guidance_ref[request], guidance)
        position = jnp.where(request_row == request, step_ref[request], position)
    sigma_now = noise_level(position.astype(jnp.float32))
    step = noise_level((position + 1).astype(jnp.float32)) - sigma_now
    lane = lax.broadcasted_iota(jnp.int32, (REQUESTS, LANES), 1)
    channels = LANES // 2
    pieces = []
    for source in range(devices):
        conditional = got_ref[pl.ds(source, REQUESTS, stride=block), :]
        unconditional = got_ref[pl.ds(REQUESTS * block + source, REQUESTS, stride=block), :]
        velocity = unconditional + guidance * (conditional - unconditional)
        first = source * block + devices
        latent_next = got_ref[first : first + REQUESTS, :] + step * velocity
        velocity_all[source] = velocity
        latent_all[source] = latent_next
        tail = jnp.where(lane < channels + 3, 1.0, 0.0)
        pieces.append(jnp.where(lane < channels, latent_next, tail))
        pieces.append(jnp.where(lane < channels, pltpu.roll(latent_next, channels, 1), tail))
    mine = lax.axis_index("seq")
    velocity = velocity_all[mine]
    latent_next = latent_all[mine]
    velocity_ref[0] = velocity[:, :channels]
    velocity_ref[1] = velocity[:, channels:]
    latent_ref[0] = latent_next[:, :channels]
    latent_ref[1] = latent_next[:, channels:]

    rounded = jnp.concatenate(pieces, axis=0).astype(jnp.bfloat16)
    rows = rounded.shape[0]
    exact = rounded.astype(jnp.float32)
    used = gram_ref.shape[0]
    image = jnp.dot(
        exact[:, :used],
        gram_ref[...],
        precision=lax.Precision.HIGHEST,
        preferred_element_type=jnp.float32,
    )
    spread = jnp.sum(image * exact[:, :used], axis=-1, keepdims=True)
    inverse = lax.rsqrt(spread * (1.0 / (HEADS * HEAD_DIM)) + 1e-06)

    request_of_row = lax.broadcasted_iota(jnp.int32, (rows, TABLE_ROWS), 0) % REQUESTS
    left = jnp.concatenate(
        [
            jnp.where(request_of_row == request, exact[:, :TABLE_ROWS], 0.0)
            for request in range(REQUESTS)
        ],
        axis=1,
    ).astype(jnp.bfloat16)
    half = half_tiles * LANES
    side = lax.axis_index("rep")

    def near(request, first, last):
        return near_ref[ids_ref[request], first:last, :]

    def far(request, first, last):
        return far_ref[request, first:last, :]

    bias_row = lax.broadcasted_iota(jnp.int32, (REQUESTS, LANES), 0)
    bias_at = half_tiles * TABLE_ROWS
    for which, take in ((side, near), (1 - side, far)):
        right = jnp.concatenate(
            [
                jnp.concatenate(
                    [
                        take(request, tile * TABLE_ROWS, (tile + 1) * TABLE_ROWS)
                        for request in range(REQUESTS)
                    ],
                    axis=0,
                )
                for tile in range(half_tiles)
            ],
            axis=1,
        )
        biases = [jnp.zeros((REQUESTS, LANES), jnp.float32)] * half_tiles
        for request in range(REQUESTS):
            block = take(request, bias_at, bias_at + BIAS_ROWS).astype(jnp.float32)
            biases = [
                jnp.where(bias_row == request, jnp.broadcast_to(block[t : t + 1], bias.shape), bias)
                for t, bias in enumerate(biases)
            ]
        bias = jnp.concatenate(biases, axis=1)
        product = jnp.dot(left, right, preferred_element_type=jnp.float32)
        product = product.reshape(rows // REQUESTS, REQUESTS, half) + bias[None]
        product_ref[:, pl.ds(pl.multiple_of(which * half, LANES), half)] = (
            product.reshape(rows, half) * inverse
        )
    shape = delta_ref.shape
    offsets = sorted({columns * target % LANES for target in range(devices)})
    own = columns * mine % LANES
    for offset in offsets:

        @pl.when(own == offset)
        def _(offset=offset):
            kept = product_ref[:, offset : offset + columns]
            delta_ref[...] = kept.astype(jnp.bfloat16).reshape(shape)


def broadcast(value, axis, source):
    kept = jnp.where(lax.axis_index(axis) == source, value, 0).astype(value.dtype)
    return lax.psum(kept, axis)


def noise_level(position):
    fraction = 1.0 - position / STEPS
    return 5.0 * fraction / (1.0 + 4.0 * fraction)


def layer_normed(rows):
    row_mean = jnp.mean(rows, axis=-1, keepdims=True)
    centered = rows - row_mean
    row_var = jnp.mean(centered * centered, axis=-1, keepdims=True)
    return centered * lax.rsqrt(row_var + 1e-06)


def many_per_stream(
    queries,
    key_states,
    value_states,
    hidden,
    residual_gate,
    head_shift,
    head_scale,
    head_weight,
    head_bias,
    guidance,
    step_index,
    lengths,
    latent,
    embed_weight,
    embed_bias,
    adapter_ids,
    adapter_down,
    adapter_up,
):
    row_count, stream_count, feature_width = queries.shape
    axis_devices = lax.axis_size("seq")
    full_length = row_count * axis_devices
    item_count = stream_count * feature_width // HEAD_DIM
    local_items = item_count // axis_devices
    score_scale = 1.0 / HEAD_DIM**0.5

    def as_items(states):
        return states.reshape(row_count, item_count, HEAD_DIM)

    query_heads, key_heads, value_heads = (
        lax.all_to_all(as_items(queries), "seq", split_axis=1, concat_axis=0, tiled=True),
        lax.all_to_all(as_items(key_states), "seq", split_axis=1, concat_axis=0, tiled=True),
        lax.all_to_all(as_items(value_states), "seq", split_axis=1, concat_axis=0, tiled=True),
    )
    first_item = lax.axis_index("seq") * local_items
    item_request = (first_item + jnp.arange(local_items)) // HEADS % REQUESTS
    selector = (item_request[:, None] == jnp.arange(REQUESTS)[None, :]).astype(jnp.int32)
    key_limit = jnp.sum(selector * lengths[None, :], axis=1)

    def attend(operands):
        query_rows, key_rows, value_rows, key_bound = operands
        scores = (
            jnp.einsum("qd,kd->qk", query_rows, key_rows, preferred_element_type=jnp.float32)
            * score_scale
        )
        allowed = jnp.arange(full_length)[None, :] < key_bound
        scores = jnp.where(allowed, scores, -jnp.inf)
        weights = jax.nn.softmax(scores, axis=-1).astype(jnp.bfloat16)
        return jnp.dot(weights, value_rows, preferred_element_type=jnp.float32).astype(jnp.bfloat16)

    attended_items = lax.map(
        attend,
        (
            jnp.moveaxis(query_heads, 1, 0),
            jnp.moveaxis(key_heads, 1, 0),
            jnp.moveaxis(value_heads, 1, 0),
            key_limit,
        ),
    )
    returned = lax.all_to_all(
        jnp.moveaxis(attended_items, 0, 1), "seq", split_axis=0, concat_axis=1, tiled=True
    )
    attended = returned.reshape(row_count, stream_count, feature_width)
    residual = hidden.astype(jnp.float32) + residual_gate[None, :, :] * attended.astype(jnp.float32)
    normed = (layer_normed(residual) * (1.0 + head_scale[None]) + head_shift[None]).astype(
        jnp.bfloat16
    )
    stream_velocity = jnp.dot(
        normed.reshape(-1, feature_width), head_weight, preferred_element_type=jnp.float32
    )
    stream_velocity = stream_velocity.reshape(row_count, stream_count, -1) + head_bias
    conditional = stream_velocity[:, :REQUESTS]
    unconditional = stream_velocity[:, REQUESTS:]
    velocity = unconditional + guidance[None, :, None] * (conditional - unconditional)
    sigma_now = noise_level(step_index.astype(jnp.float32))
    sigma_next = noise_level((step_index + 1).astype(jnp.float32))
    latent_next = latent + (sigma_next - sigma_now)[None, :, None] * velocity
    latent_rounded = latent_next.astype(jnp.bfloat16)
    held_slots = adapter_down.shape[0]
    embedded = jnp.dot(
        latent_rounded.reshape(row_count * REQUESTS, -1),
        embed_weight,
        preferred_element_type=jnp.float32,
    )
    embedded = embedded.reshape(row_count, REQUESTS, feature_width) + embed_bias
    block_input = layer_normed(embedded).astype(jnp.bfloat16)
    up_parts = lax.all_to_all(adapter_up, "seq", split_axis=1, concat_axis=0, tiled=True)
    user_count = up_parts.shape[0]
    chooser = (adapter_ids[:, None] == jnp.arange(user_count)[None, :]).astype(jnp.bfloat16)
    up_used = jnp.einsum(
        "ru,uck->rck", chooser, up_parts, preferred_element_type=jnp.float32
    ).astype(jnp.bfloat16)
    down_list = []
    for request in range(REQUESTS):
        owner_device = adapter_ids[request] // held_slots
        owner_slot = adapter_ids[request] % held_slots
        own_down = lax.dynamic_index_in_dim(adapter_down, owner_slot, 0, keepdims=False)
        whole_down = broadcast(own_down, "seq", owner_device)
        down_list.append(whole_down)
    down_used = jnp.stack(down_list, axis=0)
    low_rank = jnp.einsum(
        "lrd,rdk->lrk", block_input, down_used, preferred_element_type=jnp.float32
    ).astype(jnp.bfloat16)
    low_rank_all = lax.all_gather(low_rank, "seq", axis=0, tiled=True)
    adapter_delta = jnp.einsum(
        "lrk,rck->lrc", low_rank_all, up_used, preferred_element_type=jnp.float32
    ).astype(jnp.bfloat16)
    return (velocity, latent_next, adapter_delta)


def whole(shape):
    return pl.BlockSpec(shape, lambda *_: (0,) * len(shape))


def one_stream_each(
    queries,
    key_states,
    value_states,
    hidden,
    residual_gate,
    head_shift,
    head_scale,
    head_weight,
    head_bias,
    guidance,
    step_index,
    lengths,
    latent,
    embed_weight,
    embed_bias,
    adapter_ids,
    adapter_down,
    adapter_up,
):
    devices = lax.axis_size("seq")
    row_count, stream_count, width = queries.shape
    columns = adapter_up.shape[1] // devices
    half_tiles = window_tiles(columns, devices) // 2
    table_rows = half_tiles * TABLE_ROWS + BIAS_ROWS
    send_rows = table_rows + 4 * (width // QUARTERS // LANES) * 8
    swap = [(0, 1), (1, 0)]
    other_ids = lax.ppermute(adapter_ids, "rep", swap)
    smem = pl.BlockSpec(memory_space=pltpu.SMEM)
    vmem = pl.BlockSpec(memory_space=pltpu.VMEM)
    anywhere = pl.BlockSpec(memory_space=pl.ANY)
    params = pltpu.CompilerParams(vmem_limit_bytes=VMEM_LIMIT)

    sources = (
        queries,
        key_states,
        value_states,
        hidden,
        embed_weight,
        embed_bias[None, :],
        adapter_down[0].T,
        adapter_up[0].T,
    )
    send, gram = pl.pallas_call(
        functools.partial(
            prepare_kernel, devices=devices, columns=columns, half_tiles=half_tiles
        ),
        out_shape=(
            jax.ShapeDtypeStruct((devices, send_rows, LANES), jnp.bfloat16),
            jax.ShapeDtypeStruct((80, 80), jnp.float32),
        ),
        in_specs=[anywhere] * len(sources),
        out_specs=(anywhere, vmem),
        scratch_shapes=[pltpu.VMEM(source.shape, source.dtype) for source in sources]
        + [
            pltpu.VMEM((devices, send_rows, LANES), jnp.bfloat16),
            pltpu.SemaphoreType.DMA((len(sources),)),
            pltpu.SemaphoreType.DMA((1 + devices,)),
        ],
        compiler_params=pltpu.CompilerParams(vmem_limit_bytes=PREPARE_VMEM_LIMIT),
        name="prepare",
    )(*sources)
    got = lax.all_to_all(send, "seq", split_axis=0, concat_axis=0, tiled=True)

    chosen = pl.pallas_call(
        choose_kernel,
        out_shape=jax.ShapeDtypeStruct((REQUESTS, table_rows, LANES), jnp.bfloat16),
        in_specs=[smem, vmem],
        out_specs=vmem,
        compiler_params=params,
        name="choose",
    )(other_ids, got)
    far = lax.ppermute(chosen, "rep", swap)

    quarter = width // QUARTERS
    channels = head_weight.shape[1]
    rows, head = pl.pallas_call(
        modulate_kernel,
        out_shape=(
            jax.ShapeDtypeStruct((3, 8, quarter), jnp.float32),
            jax.ShapeDtypeStruct((QUARTERS * channels, quarter), head_weight.dtype),
        ),
        in_specs=[vmem] * 4,
        out_specs=(vmem, vmem),
        compiler_params=params,
        name="modulate",
    )(residual_gate, head_shift, head_scale, head_weight.T)
    payload_rows = devices + REQUESTS
    payload = pl.pallas_call(
        functools.partial(attend_kernel, table_rows=table_rows),
        out_shape=jax.ShapeDtypeStruct((devices, payload_rows, LANES), jnp.float32),
        in_specs=[smem] + [vmem] * 5,
        out_specs=vmem,
        scratch_shapes=[
            pltpu.VMEM((quarter // LANES, devices * 8, LANES), jnp.float32),
            pltpu.VMEM((devices * 8, LANES), jnp.float32),
        ],
        compiler_params=params,
        name="attend",
        cost_estimate=pl.CostEstimate(
            flops=10**9, bytes_accessed=4 * 10**6, transcendentals=2 * 10**5
        ),
    )(
        lengths,
        got,
        rows,
        head,
        head_bias[None, :],
        latent,
    )
    shared = lax.all_to_all(payload, "seq", split_axis=0, concat_axis=0, tiled=True)

    across = (REQUESTS, LANES)
    return pl.pallas_call(
        functools.partial(finish_kernel, devices=devices, columns=columns, half_tiles=half_tiles),
        out_shape=(
            jax.ShapeDtypeStruct(latent.shape, jnp.float32),
            jax.ShapeDtypeStruct(latent.shape, jnp.float32),
            jax.ShapeDtypeStruct((row_count * devices, REQUESTS, columns), jnp.bfloat16),
        ),
        in_specs=[smem, vmem, smem, smem] + [vmem] * 3,
        out_specs=(vmem, vmem, vmem),
        scratch_shapes=[
            pltpu.VMEM((devices,) + across, jnp.float32),
            pltpu.VMEM((devices,) + across, jnp.float32),
            pltpu.VMEM((row_count * devices * REQUESTS, 2 * half_tiles * LANES), jnp.float32),
        ],
        compiler_params=params,
        name="finish",
    )(
        adapter_ids,
        shared.reshape(devices * payload_rows, LANES),
        guidance,
        step_index,
        gram,
        got,
        far,
    )


def window_tiles(columns, devices):
    most = max(
        pl.cdiv(columns * (d + 1), LANES) - columns * d // LANES for d in range(devices)
    )
    return (most + 1) // 2 * 2


def shards(*operands):
    queries, held, table = operands[0], operands[16], operands[17]
    row_count, stream_count, width = queries.shape
    devices = lax.axis_size("seq")
    columns = table.shape[1] // devices
    fits = (
        stream_count == devices
        and row_count == 2
        and held.shape[0] == 1
        and held.shape[2] == LANES // 2
        and lax.axis_size("rep") == 2
        and width % (QUARTERS * LANES) == 0
        and all(
            columns * d // LANES + window_tiles(columns, devices) <= table.shape[1] // LANES
            for d in range(devices)
        )
    )
    return one_stream_each(*operands) if fits else many_per_stream(*operands)


def solution(mesh):
    placed = (
        P("seq", "rep", None),
        P("seq", "rep", None),
        P("seq", "rep", None),
        P("seq", "rep", None),
        P("rep", None),
        P("rep", None),
        P("rep", None),
        P(),
        P(),
        P("rep"),
        P("rep"),
        P("rep"),
        P("seq", "rep", None),
        P(),
        P(),
        P("rep"),
        P("seq", None, None),
        P("seq", None, None),
    )
    return jax.shard_map(
        shards,
        mesh=mesh,
        in_specs=placed,
        out_specs=(P("seq", "rep", None), P("seq", "rep", None), P(None, "rep", "seq")),
        check_vma=False,
    )
```

```python
import functools

import jax
import jax.numpy as jnp
from jax import lax
from jax.experimental import pallas as pl
from jax.experimental.pallas import tpu as pltpu
from jax.sharding import PartitionSpec as P

HEADS = 40
HEAD_DIM = 128
REQUESTS = 8
STEPS = 10
LANES = 128
QUARTERS = 4
TABLE_ROWS = 64
BIAS_ROWS = 8
LATENT_ROW = 4
VMEM_LIMIT = 20 << 20
PREPARE_VMEM_LIMIT = 56 << 20

NT = (((1,), (1,)), ((), ()))


def nt_dot(a, b):
    return lax.dot_general(a, b, NT, preferred_element_type=jnp.float32)


def prepare_kernel(*refs, devices, columns, half_tiles):
    sources, (sent_ref, gram_ref), held = refs[:9], refs[9:11], refs[11:20]
    send_ref, sems, out_sems = refs[20:]
    copies = [
        pltpu.make_async_copy(source, target, sems.at[index])
        for index, (source, target) in enumerate(zip(sources, held))
    ]
    for copy in copies:
        copy.start()
    q_ref, k_ref, v_ref, h_ref, embed_ref, bias_ref, down_ref, latent_ref, up_ref = held
    row_count, stream_count, width = q_ref.shape
    quarter = width // QUARTERS
    tiles = quarter // LANES
    table_rows = half_tiles * TABLE_ROWS + BIAS_ROWS
    size = stream_count * 8
    to = lax.broadcasted_iota(jnp.int32, (size, size), 0)
    at = lax.broadcasted_iota(jnp.int32, (size, size), 1)
    same = (to // 8 == at % stream_count) & (to % 8 == at // stream_count)
    permutation = jnp.where(same, 1.0, 0.0).astype(jnp.bfloat16)
    for kind, ref in enumerate((q_ref, k_ref, v_ref, h_ref)):
        copies[kind].wait()
        stacked = jnp.concatenate(
            [
                ref[token, :, part * quarter : (part + 1) * quarter]
                for part in range(QUARTERS)
                for token in range(row_count)
            ],
            axis=0,
        )
        moved = jnp.dot(permutation, stacked, preferred_element_type=jnp.float32)
        moved = moved.astype(jnp.bfloat16)
        for tile in range(tiles):
            first = table_rows + (kind * tiles + tile) * 8
            send_ref[:, first : first + 8, :] = moved[
                :, tile * LANES : (tile + 1) * LANES
            ].reshape(stream_count, 8, LANES)

    writes = [
        pltpu.make_async_copy(
            send_ref.at[:, table_rows:], sent_ref.at[:, table_rows:], out_sems.at[0]
        )
    ]
    writes[0].start()

    for copy in copies[4:8]:
        copy.wait()
    bias = bias_ref[...]
    high = bias.astype(jnp.bfloat16).astype(jnp.float32)
    middle = (bias - high).astype(jnp.bfloat16).astype(jnp.float32)
    low = bias - high - middle
    row = lax.broadcasted_iota(jnp.int32, (16, width), 0)
    extra = jnp.where(row == 0, high, jnp.where(row == 1, middle, jnp.where(row == 2, low, 0.0)))
    extra = jnp.where(row == 3, 1.0, extra).astype(jnp.bfloat16)
    rows = jnp.concatenate([embed_ref[...], extra], axis=0)
    raw = nt_dot(rows, down_ref[...])
    gram = nt_dot(rows, rows)
    ones_at = 67
    sums = gram[:, ones_at : ones_at + 1]
    centered = raw - sums * (1.0 / width) * raw[ones_at : ones_at + 1, :]
    gram = gram - sums * (1.0 / width) * gram[ones_at : ones_at + 1, :]
    gram = jnp.concatenate([gram, jnp.zeros((80, LANES - 80), jnp.float32)], axis=1)
    gram_high = gram.astype(jnp.bfloat16)
    left_over = gram - gram_high.astype(jnp.float32)
    gram_middle = left_over.astype(jnp.bfloat16)
    gram_low = (left_over - gram_middle.astype(jnp.float32)).astype(jnp.bfloat16)
    gram_ref[...] = jnp.concatenate([gram_high, gram_middle, gram_low], axis=1)
    bias_row = centered[64:65] + centered[65:66] + centered[66:67]
    tail = lax.broadcasted_iota(jnp.int32, (8, centered.shape[1]), 0)
    mixing = jnp.concatenate(
        [centered[:64], jnp.where(tail == 0, jnp.broadcast_to(bias_row, tail.shape), 0.0)], axis=0
    )
    mixing_high = mixing.astype(jnp.bfloat16)
    mixing_low = (mixing - mixing_high.astype(jnp.float32)).astype(jnp.bfloat16)
    mixing = jnp.concatenate([mixing_high, mixing_low], axis=1)

    half = half_tiles * LANES
    side = lax.axis_index("rep") * half
    copies[8].wait()
    latent = jnp.concatenate([latent_ref[0], latent_ref[1]], axis=1)
    latent_high = latent.astype(jnp.bfloat16).astype(jnp.float32)
    latent_middle = (latent - latent_high).astype(jnp.bfloat16).astype(jnp.float32)
    latent_pieces = (latent_high, latent_middle, latent - latent_high - latent_middle)
    row = lax.broadcasted_iota(jnp.int32, (BIAS_ROWS, LANES), 0)
    for target in range(devices):
        start = columns * target // LANES * LANES
        part = up_ref[:, pl.ds(pl.multiple_of(start + side, LANES), half)]
        table = jnp.dot(
            mixing, jnp.concatenate([part, part], axis=0), preferred_element_type=jnp.float32
        )
        biases = jnp.zeros((BIAS_ROWS, LANES), jnp.float32)
        for tile in range(half_tiles):
            piece = table[:, tile * LANES : (tile + 1) * LANES]
            send_ref[target, tile * TABLE_ROWS : (tile + 1) * TABLE_ROWS, :] = piece[
                :TABLE_ROWS
            ].astype(jnp.bfloat16)
            biases = jnp.where(
                row == tile,
                jnp.broadcast_to(piece[TABLE_ROWS : TABLE_ROWS + 1], biases.shape),
                biases,
            )
        request = target % REQUESTS
        for index, piece in enumerate(latent_pieces):
            biases = jnp.where(
                row == LATENT_ROW + index,
                jnp.broadcast_to(piece[request : request + 1], biases.shape),
                biases,
            )
        send_ref[target, half_tiles * TABLE_ROWS : table_rows, :] = biases.astype(jnp.bfloat16)
        writes.append(
            pltpu.make_async_copy(
                send_ref.at[target, 0:table_rows],
                sent_ref.at[target, 0:table_rows],
                out_sems.at[1 + target],
            )
        )
        writes[-1].start()
    for write in writes:
        write.wait()


def choose_kernel(ids_ref, got_ref, out_ref):
    count = out_ref.shape[1]
    for request in range(REQUESTS):
        out_ref[request] = got_ref[ids_ref[request], 0:count, :]


def group_sum(x):
    grouped = x.reshape(x.shape[0] // 8, 8, x.shape[1])
    grouped = grouped + pltpu.roll(grouped, 2, 1)
    grouped = grouped + pltpu.roll(grouped, 4, 1)
    return grouped.reshape(x.shape)


def modulate_kernel(gate_ref, shift_ref, scale_ref, weight_ref, rows_ref, head_ref):
    width = gate_ref.shape[1]
    quarter = width // QUARTERS
    mine = lax.axis_index("seq")
    part_of_row = lax.broadcasted_iota(jnp.int32, (8, quarter), 0) // 2
    for index, ref in enumerate((gate_ref, shift_ref, scale_ref)):
        block = ref[pl.ds(pl.multiple_of(mine // 8 * 8, 8), 8), :]
        row = pltpu.roll(block, (8 - mine % 8) % 8, 0)[0:1]
        value = jnp.zeros((8, quarter), jnp.float32)
        for part in range(QUARTERS):
            piece = row[:, part * quarter : (part + 1) * quarter]
            value = jnp.where(part_of_row == part, jnp.broadcast_to(piece, value.shape), value)
        rows_ref[index] = value
    channels = weight_ref.shape[0]
    for part in range(QUARTERS):
        head_ref[part * channels : (part + 1) * channels, :] = weight_ref[
            :, part * quarter : (part + 1) * quarter
        ]


def sigma_change(position):
    now = noise_level(position.astype(jnp.float32))
    return noise_level((position + 1).astype(jnp.float32)) - now


def attend_kernel(
    lengths_ref,
    guidance_ref,
    step_ref,
    got_ref,
    rows_ref,
    head_ref,
    bias_ref,
    out_ref,
    residual_ref,
    pick_ref,
    *,
    table_rows,
):
    devices = got_ref.shape[0]
    quarter = rows_ref.shape[2]
    width = quarter * QUARTERS
    tiles = quarter // LANES
    size = devices * 8
    mine = lax.axis_index("seq")
    limit = lengths_ref[mine % REQUESTS]
    score_scale = 1.0 / HEAD_DIM**0.5

    row = lax.broadcasted_iota(jnp.int32, (size, size), 0)
    column = lax.broadcasted_iota(jnp.int32, (size, size), 1)
    key_token = column // 8 * 2 + column % 2
    allowed = (row % 8 // 2 == column % 8 // 2) & (key_token < limit)

    def modulation(index, tile):
        value = rows_ref[index, :, tile * LANES : (tile + 1) * LANES]
        return jnp.broadcast_to(value[None], (devices, 8, LANES)).reshape(size, LANES)

    total = jnp.zeros((size, LANES), jnp.float32)
    for tile in range(tiles):
        q, k, v, h = [
            got_ref[
                :,
                table_rows + (kind * tiles + tile) * 8 : table_rows + (kind * tiles + tile) * 8 + 8,
                :,
            ].reshape(size, LANES)
            for kind in range(4)
        ]
        scores = jnp.where(allowed, nt_dot(q, k) * score_scale, -jnp.inf)
        peak = jnp.max(scores, axis=-1, keepdims=True)
        raised = jnp.exp(scores - peak)
        weights = raised / jnp.sum(raised, axis=-1, keepdims=True)
        attended = jnp.dot(
            weights.astype(jnp.bfloat16), v, preferred_element_type=jnp.float32
        ).astype(jnp.bfloat16)
        residual = h.astype(jnp.float32) + modulation(0, tile) * attended.astype(jnp.float32)
        residual_ref[tile] = residual
        total = total + residual
    mean = jnp.sum(group_sum(total), axis=-1, keepdims=True) * (1.0 / width)
    total = jnp.zeros((size, LANES), jnp.float32)
    for tile in range(tiles):
        centered = residual_ref[tile] - mean
        residual_ref[tile] = centered
        total = total + centered * centered
    variance = jnp.sum(group_sum(total), axis=-1, keepdims=True) * (1.0 / width)
    inverse = lax.rsqrt(variance + 1e-06)
    channels = head_ref.shape[0] // QUARTERS
    product = jnp.zeros((size, QUARTERS * channels), jnp.float32)
    for tile in range(tiles):
        normed = residual_ref[tile] * inverse * (1.0 + modulation(2, tile)) + modulation(1, tile)
        product = product + nt_dot(
            normed.astype(jnp.bfloat16), head_ref[:, tile * LANES : (tile + 1) * LANES]
        )
    row = lax.broadcasted_iota(jnp.int32, product.shape, 0)
    column = lax.broadcasted_iota(jnp.int32, product.shape, 1)
    product = jnp.where(row % 8 // 2 == column // channels, product, 0.0)
    product = group_sum(product[:, :LANES] + product[:, LANES:])
    product = product + pltpu.roll(product, channels, 1)
    bias = bias_ref[...]
    product = product + jnp.concatenate([bias, bias], axis=1)
    pick_ref[...] = product
    first_token = pick_ref[pl.ds(0, devices, stride=8), :]
    second_token = pick_ref[pl.ds(1, devices, stride=8), :]
    lane = lax.broadcasted_iota(jnp.int32, (devices, LANES), 1)
    stream_velocity = jnp.where(lane < channels, first_token, second_token)
    pieces = got_ref[:, table_rows - BIAS_ROWS : table_rows, :].astype(jnp.float32)
    latent = sum(pieces[:, LATENT_ROW + index, :] for index in range(3))
    guidance = jnp.full((devices, LANES), guidance_ref[mine % REQUESTS], jnp.float32)
    change = sigma_change(jnp.full((devices, LANES), step_ref[mine % REQUESTS], jnp.int32))
    conditional = latent + change * guidance * stream_velocity
    unconditional = change * (1.0 - guidance) * stream_velocity
    block = jnp.where(jnp.full((devices, LANES), mine, jnp.int32) < REQUESTS, conditional, unconditional)
    out_ref[...] = jnp.broadcast_to(block[None], out_ref.shape)


def finish_kernel(
    ids_ref,
    got_ref,
    step_ref,
    own_ref,
    gram_ref,
    near_ref,
    far_ref,
    velocity_ref,
    latent_ref,
    delta_ref,
    latent_all,
    product_ref,
    *,
    devices,
    columns,
    half_tiles,
):
    block = devices
    request_row = lax.broadcasted_iota(jnp.int32, (REQUESTS, LANES), 0)
    position = jnp.zeros((REQUESTS, LANES), jnp.int32)
    for request in range(REQUESTS):
        position = jnp.where(request_row == request, step_ref[request], position)
    change = sigma_change(position)
    lane = lax.broadcasted_iota(jnp.int32, (REQUESTS, LANES), 1)
    channels = LANES // 2
    pieces = []
    for source in range(devices):
        conditional = got_ref[pl.ds(source, REQUESTS, stride=block), :]
        unconditional = got_ref[pl.ds(REQUESTS * block + source, REQUESTS, stride=block), :]
        latent_next = conditional + unconditional
        latent_all[source] = latent_next
        tail = jnp.where(lane < channels + 3, 1.0, 0.0)
        pieces.append(jnp.where(lane < channels, latent_next, tail))
        pieces.append(jnp.where(lane < channels, pltpu.roll(latent_next, channels, 1), tail))
    mine = lax.axis_index("seq")
    latent_next = latent_all[mine]
    own = jnp.concatenate([own_ref[0], own_ref[1]], axis=1)
    velocity = (latent_next - own) / change
    velocity_ref[0] = velocity[:, :channels]
    velocity_ref[1] = velocity[:, channels:]
    latent_ref[0] = latent_next[:, :channels]
    latent_ref[1] = latent_next[:, channels:]

    rounded = jnp.concatenate(pieces, axis=0).astype(jnp.bfloat16)
    rows = rounded.shape[0]
    exact = rounded.astype(jnp.float32)
    used = gram_ref.shape[0]
    pieces = jnp.dot(rounded[:, :used], gram_ref[...], preferred_element_type=jnp.float32)
    image = pieces[:, :LANES] + pieces[:, LANES : 2 * LANES] + pieces[:, 2 * LANES :]
    spread = jnp.sum(image * exact, axis=-1, keepdims=True)
    inverse = lax.rsqrt(spread * (1.0 / (HEADS * HEAD_DIM)) + 1e-06)

    row = lax.broadcasted_iota(jnp.int32, (rows, LANES), 0) % REQUESTS
    column = lax.broadcasted_iota(jnp.int32, (rows, LANES), 1)
    twice = jnp.where(column < channels, exact, pltpu.roll(exact, channels, 1))
    request_here = row - jnp.where(column < channels, 0, 1)
    left = jnp.concatenate(
        [
            jnp.where(request_here == request, twice, 0.0).astype(jnp.bfloat16)
            for request in range(0, REQUESTS, 2)
        ],
        axis=1,
    )
    half = half_tiles * LANES
    side = lax.axis_index("rep")

    def near(request, first, last):
        return near_ref[ids_ref[request], first:last, :]

    def far(request, first, last):
        return far_ref[request, first:last, :]

    bias_row = lax.broadcasted_iota(jnp.int32, (REQUESTS, LANES), 0)
    bias_at = half_tiles * TABLE_ROWS
    for which, take in ((side, near), (1 - side, far)):
        right = jnp.concatenate(
            [
                jnp.concatenate(
                    [
                        take(request, tile * TABLE_ROWS, (tile + 1) * TABLE_ROWS)
                        for request in range(REQUESTS)
                    ],
                    axis=0,
                )
                for tile in range(half_tiles)
            ],
            axis=1,
        )
        biases = [jnp.zeros((REQUESTS, LANES), jnp.float32)] * half_tiles
        for request in range(REQUESTS):
            block = take(request, bias_at, bias_at + BIAS_ROWS).astype(jnp.float32)
            biases = [
                jnp.where(bias_row == request, jnp.broadcast_to(block[t : t + 1], bias.shape), bias)
                for t, bias in enumerate(biases)
            ]
        bias = jnp.concatenate(biases, axis=1)
        product = jnp.dot(left, right, preferred_element_type=jnp.float32)
        product = product.reshape(rows // REQUESTS, REQUESTS, half) + bias[None]
        product_ref[:, pl.ds(pl.multiple_of(which * half, LANES), half)] = (
            product.reshape(rows, half) * inverse
        )
    shape = delta_ref.shape
    offsets = sorted({columns * target % LANES for target in range(devices)})
    own = columns * mine % LANES
    for offset in offsets:

        @pl.when(own == offset)
        def _(offset=offset):
            kept = product_ref[:, offset : offset + columns]
            delta_ref[...] = kept.astype(jnp.bfloat16).reshape(shape)


def broadcast(value, axis, source):
    kept = jnp.where(lax.axis_index(axis) == source, value, 0).astype(value.dtype)
    return lax.psum(kept, axis)


def noise_level(position):
    fraction = 1.0 - position / STEPS
    return 5.0 * fraction / (1.0 + 4.0 * fraction)


def layer_normed(rows):
    row_mean = jnp.mean(rows, axis=-1, keepdims=True)
    centered = rows - row_mean
    row_var = jnp.mean(centered * centered, axis=-1, keepdims=True)
    return centered * lax.rsqrt(row_var + 1e-06)


def many_per_stream(
    queries,
    key_states,
    value_states,
    hidden,
    residual_gate,
    head_shift,
    head_scale,
    head_weight,
    head_bias,
    guidance,
    step_index,
    lengths,
    latent,
    embed_weight,
    embed_bias,
    adapter_ids,
    adapter_down,
    adapter_up,
):
    row_count, stream_count, feature_width = queries.shape
    axis_devices = lax.axis_size("seq")
    full_length = row_count * axis_devices
    item_count = stream_count * feature_width // HEAD_DIM
    local_items = item_count // axis_devices
    score_scale = 1.0 / HEAD_DIM**0.5

    def as_items(states):
        return states.reshape(row_count, item_count, HEAD_DIM)

    query_heads, key_heads, value_heads = (
        lax.all_to_all(as_items(queries), "seq", split_axis=1, concat_axis=0, tiled=True),
        lax.all_to_all(as_items(key_states), "seq", split_axis=1, concat_axis=0, tiled=True),
        lax.all_to_all(as_items(value_states), "seq", split_axis=1, concat_axis=0, tiled=True),
    )
    first_item = lax.axis_index("seq") * local_items
    item_request = (first_item + jnp.arange(local_items)) // HEADS % REQUESTS
    selector = (item_request[:, None] == jnp.arange(REQUESTS)[None, :]).astype(jnp.int32)
    key_limit = jnp.sum(selector * lengths[None, :], axis=1)

    def attend(operands):
        query_rows, key_rows, value_rows, key_bound = operands
        scores = (
            jnp.einsum("qd,kd->qk", query_rows, key_rows, preferred_element_type=jnp.float32)
            * score_scale
        )
        allowed = jnp.arange(full_length)[None, :] < key_bound
        scores = jnp.where(allowed, scores, -jnp.inf)
        weights = jax.nn.softmax(scores, axis=-1).astype(jnp.bfloat16)
        return jnp.dot(weights, value_rows, preferred_element_type=jnp.float32).astype(jnp.bfloat16)

    attended_items = lax.map(
        attend,
        (
            jnp.moveaxis(query_heads, 1, 0),
            jnp.moveaxis(key_heads, 1, 0),
            jnp.moveaxis(value_heads, 1, 0),
            key_limit,
        ),
    )
    returned = lax.all_to_all(
        jnp.moveaxis(attended_items, 0, 1), "seq", split_axis=0, concat_axis=1, tiled=True
    )
    attended = returned.reshape(row_count, stream_count, feature_width)
    residual = hidden.astype(jnp.float32) + residual_gate[None, :, :] * attended.astype(jnp.float32)
    normed = (layer_normed(residual) * (1.0 + head_scale[None]) + head_shift[None]).astype(
        jnp.bfloat16
    )
    stream_velocity = jnp.dot(
        normed.reshape(-1, feature_width), head_weight, preferred_element_type=jnp.float32
    )
    stream_velocity = stream_velocity.reshape(row_count, stream_count, -1) + head_bias
    conditional = stream_velocity[:, :REQUESTS]
    unconditional = stream_velocity[:, REQUESTS:]
    velocity = unconditional + guidance[None, :, None] * (conditional - unconditional)
    sigma_now = noise_level(step_index.astype(jnp.float32))
    sigma_next = noise_level((step_index + 1).astype(jnp.float32))
    latent_next = latent + (sigma_next - sigma_now)[None, :, None] * velocity
    latent_rounded = latent_next.astype(jnp.bfloat16)
    held_slots = adapter_down.shape[0]
    embedded = jnp.dot(
        latent_rounded.reshape(row_count * REQUESTS, -1),
        embed_weight,
        preferred_element_type=jnp.float32,
    )
    embedded = embedded.reshape(row_count, REQUESTS, feature_width) + embed_bias
    block_input = layer_normed(embedded).astype(jnp.bfloat16)
    up_parts = lax.all_to_all(adapter_up, "seq", split_axis=1, concat_axis=0, tiled=True)
    user_count = up_parts.shape[0]
    chooser = (adapter_ids[:, None] == jnp.arange(user_count)[None, :]).astype(jnp.bfloat16)
    up_used = jnp.einsum(
        "ru,uck->rck", chooser, up_parts, preferred_element_type=jnp.float32
    ).astype(jnp.bfloat16)
    down_list = []
    for request in range(REQUESTS):
        owner_device = adapter_ids[request] // held_slots
        owner_slot = adapter_ids[request] % held_slots
        own_down = lax.dynamic_index_in_dim(adapter_down, owner_slot, 0, keepdims=False)
        whole_down = broadcast(own_down, "seq", owner_device)
        down_list.append(whole_down)
    down_used = jnp.stack(down_list, axis=0)
    low_rank = jnp.einsum(
        "lrd,rdk->lrk", block_input, down_used, preferred_element_type=jnp.float32
    ).astype(jnp.bfloat16)
    low_rank_all = lax.all_gather(low_rank, "seq", axis=0, tiled=True)
    adapter_delta = jnp.einsum(
        "lrk,rck->lrc", low_rank_all, up_used, preferred_element_type=jnp.float32
    ).astype(jnp.bfloat16)
    return (velocity, latent_next, adapter_delta)


def whole(shape):
    return pl.BlockSpec(shape, lambda *_: (0,) * len(shape))


def one_stream_each(
    queries,
    key_states,
    value_states,
    hidden,
    residual_gate,
    head_shift,
    head_scale,
    head_weight,
    head_bias,
    guidance,
    step_index,
    lengths,
    latent,
    embed_weight,
    embed_bias,
    adapter_ids,
    adapter_down,
    adapter_up,
):
    devices = lax.axis_size("seq")
    row_count, stream_count, width = queries.shape
    columns = adapter_up.shape[1] // devices
    half_tiles = window_tiles(columns, devices) // 2
    table_rows = half_tiles * TABLE_ROWS + BIAS_ROWS
    send_rows = table_rows + 4 * (width // QUARTERS // LANES) * 8
    swap = [(0, 1), (1, 0)]
    other_ids = lax.ppermute(adapter_ids, "rep", swap)
    smem = pl.BlockSpec(memory_space=pltpu.SMEM)
    vmem = pl.BlockSpec(memory_space=pltpu.VMEM)
    anywhere = pl.BlockSpec(memory_space=pl.ANY)
    params = pltpu.CompilerParams(vmem_limit_bytes=VMEM_LIMIT)

    sources = (
        queries,
        key_states,
        value_states,
        hidden,
        embed_weight,
        embed_bias[None, :],
        adapter_down[0].T,
        latent,
        adapter_up[0].T,
    )
    send, gram = pl.pallas_call(
        functools.partial(
            prepare_kernel, devices=devices, columns=columns, half_tiles=half_tiles
        ),
        out_shape=(
            jax.ShapeDtypeStruct((devices, send_rows, LANES), jnp.bfloat16),
            jax.ShapeDtypeStruct((80, 3 * LANES), jnp.bfloat16),
        ),
        in_specs=[anywhere] * len(sources),
        out_specs=(anywhere, vmem),
        scratch_shapes=[pltpu.VMEM(source.shape, source.dtype) for source in sources]
        + [
            pltpu.VMEM((devices, send_rows, LANES), jnp.bfloat16),
            pltpu.SemaphoreType.DMA((len(sources),)),
            pltpu.SemaphoreType.DMA((1 + devices,)),
        ],
        compiler_params=pltpu.CompilerParams(vmem_limit_bytes=PREPARE_VMEM_LIMIT),
        name="prepare",
    )(*sources)
    got = lax.all_to_all(send, "seq", split_axis=0, concat_axis=0, tiled=True)

    chosen = pl.pallas_call(
        choose_kernel,
        out_shape=jax.ShapeDtypeStruct((REQUESTS, table_rows, LANES), jnp.bfloat16),
        in_specs=[smem, vmem],
        out_specs=vmem,
        compiler_params=params,
        name="choose",
    )(other_ids, got)
    far = lax.ppermute(chosen, "rep", swap)

    quarter = width // QUARTERS
    channels = head_weight.shape[1]
    rows, head = pl.pallas_call(
        modulate_kernel,
        out_shape=(
            jax.ShapeDtypeStruct((3, 8, quarter), jnp.float32),
            jax.ShapeDtypeStruct((QUARTERS * channels, quarter), head_weight.dtype),
        ),
        in_specs=[vmem] * 4,
        out_specs=(vmem, vmem),
        compiler_params=params,
        name="modulate",
    )(residual_gate, head_shift, head_scale, head_weight.T)
    payload_rows = devices
    payload = pl.pallas_call(
        functools.partial(attend_kernel, table_rows=table_rows),
        out_shape=jax.ShapeDtypeStruct((devices, payload_rows, LANES), jnp.float32),
        in_specs=[smem] * 3 + [vmem] * 4,
        out_specs=vmem,
        scratch_shapes=[
            pltpu.VMEM((quarter // LANES, devices * 8, LANES), jnp.float32),
            pltpu.VMEM((devices * 8, LANES), jnp.float32),
        ],
        compiler_params=params,
        name="attend",
        cost_estimate=pl.CostEstimate(
            flops=10**9, bytes_accessed=4 * 10**6, transcendentals=2 * 10**5
        ),
    )(
        lengths,
        guidance,
        step_index,
        got,
        rows,
        head,
        head_bias[None, :],
    )
    shared = lax.all_to_all(payload, "seq", split_axis=0, concat_axis=0, tiled=True)

    across = (REQUESTS, LANES)
    return pl.pallas_call(
        functools.partial(finish_kernel, devices=devices, columns=columns, half_tiles=half_tiles),
        out_shape=(
            jax.ShapeDtypeStruct(latent.shape, jnp.float32),
            jax.ShapeDtypeStruct(latent.shape, jnp.float32),
            jax.ShapeDtypeStruct((row_count * devices, REQUESTS, columns), jnp.bfloat16),
        ),
        in_specs=[smem, vmem, smem] + [vmem] * 4,
        out_specs=(vmem, vmem, vmem),
        scratch_shapes=[
            pltpu.VMEM((devices,) + across, jnp.float32),
            pltpu.VMEM((row_count * devices * REQUESTS, 2 * half_tiles * LANES), jnp.float32),
        ],
        compiler_params=params,
        name="finish",
    )(
        adapter_ids,
        shared.reshape(devices * payload_rows, LANES),
        step_index,
        latent,
        gram,
        got,
        far,
    )


def window_tiles(columns, devices):
    most = max(
        pl.cdiv(columns * (d + 1), LANES) - columns * d // LANES for d in range(devices)
    )
    return (most + 1) // 2 * 2


def shards(*operands):
    queries, held, table = operands[0], operands[16], operands[17]
    row_count, stream_count, width = queries.shape
    devices = lax.axis_size("seq")
    columns = table.shape[1] // devices
    fits = (
        stream_count == devices
        and row_count == 2
        and held.shape[0] == 1
        and held.shape[2] == LANES // 2
        and lax.axis_size("rep") == 2
        and window_tiles(columns, devices) // 2 <= LATENT_ROW
        and width % (QUARTERS * LANES) == 0
        and all(
            columns * d // LANES + window_tiles(columns, devices) <= table.shape[1] // LANES
            for d in range(devices)
        )
    )
    return one_stream_each(*operands) if fits else many_per_stream(*operands)


def solution(mesh):
    placed = (
        P("seq", "rep", None),
        P("seq", "rep", None),
        P("seq", "rep", None),
        P("seq", "rep", None),
        P("rep", None),
        P("rep", None),
        P("rep", None),
        P(),
        P(),
        P("rep"),
        P("rep"),
        P("rep"),
        P("seq", "rep", None),
        P(),
        P(),
        P("rep"),
        P("seq", None, None),
        P("seq", None, None),
    )
    return jax.shard_map(
        shards,
        mesh=mesh,
        in_specs=placed,
        out_specs=(P("seq", "rep", None), P("seq", "rep", None), P(None, "rep", "seq")),
        check_vma=False,
    )
```

```python
import functools

import jax
import jax.numpy as jnp
from jax import lax
from jax.experimental import pallas as pl
from jax.experimental.pallas import tpu as pltpu
from jax.sharding import PartitionSpec as P

HEADS = 40
HEAD_DIM = 128
REQUESTS = 8
STEPS = 10
LANES = 128
QUARTERS = 4
TABLE_ROWS = 64
BIAS_ROWS = 8
LATENT_ROW = 4
TOGETHER = 5
VMEM_LIMIT = 20 << 20
PREPARE_VMEM_LIMIT = 56 << 20

NT = (((1,), (1,)), ((), ()))


def nt_dot(a, b):
    return lax.dot_general(a, b, NT, preferred_element_type=jnp.float32)


def prepare_kernel(*refs, devices, columns, half_tiles):
    sources, (sent_ref, gram_ref), held = refs[:9], refs[9:11], refs[11:20]
    send_ref, sems, out_sems = refs[20:]
    copies = [
        pltpu.make_async_copy(source, target, sems.at[index])
        for index, (source, target) in enumerate(zip(sources, held))
    ]
    for copy in copies:
        copy.start()
    q_ref, k_ref, v_ref, h_ref, embed_ref, bias_ref, down_ref, latent_ref, up_ref = held
    row_count, stream_count, width = q_ref.shape
    quarter = width // QUARTERS
    tiles = quarter // LANES
    table_rows = half_tiles * TABLE_ROWS + BIAS_ROWS
    size = stream_count * 8
    to = lax.broadcasted_iota(jnp.int32, (size, size), 0)
    at = lax.broadcasted_iota(jnp.int32, (size, size), 1)
    same = (to // 8 == at % stream_count) & (to % 8 == at // stream_count)
    permutation = jnp.where(same, 1.0, 0.0).astype(jnp.bfloat16)
    for kind, ref in enumerate((q_ref, k_ref, v_ref, h_ref)):
        copies[kind].wait()
        stacked = jnp.concatenate(
            [
                ref[token, :, part * quarter : (part + 1) * quarter]
                for part in range(QUARTERS)
                for token in range(row_count)
            ],
            axis=0,
        )
        moved = jnp.dot(permutation, stacked, preferred_element_type=jnp.float32)
        moved = moved.astype(jnp.bfloat16)
        for tile in range(tiles):
            first = table_rows + (kind * tiles + tile) * 8
            send_ref[:, first : first + 8, :] = moved[
                :, tile * LANES : (tile + 1) * LANES
            ].reshape(stream_count, 8, LANES)

    writes = [
        pltpu.make_async_copy(
            send_ref.at[:, table_rows:], sent_ref.at[:, table_rows:], out_sems.at[0]
        )
    ]
    writes[0].start()

    for copy in copies[4:8]:
        copy.wait()
    bias = bias_ref[...]
    high = bias.astype(jnp.bfloat16).astype(jnp.float32)
    middle = (bias - high).astype(jnp.bfloat16).astype(jnp.float32)
    low = bias - high - middle
    row = lax.broadcasted_iota(jnp.int32, (16, width), 0)
    extra = jnp.where(row == 0, high, jnp.where(row == 1, middle, jnp.where(row == 2, low, 0.0)))
    extra = jnp.where(row == 3, 1.0, extra).astype(jnp.bfloat16)
    rows = jnp.concatenate([embed_ref[...], extra], axis=0)
    raw = nt_dot(rows, down_ref[...])
    gram = nt_dot(rows, rows)
    ones_at = 67
    sums = gram[:, ones_at : ones_at + 1]
    centered = raw - sums * (1.0 / width) * raw[ones_at : ones_at + 1, :]
    gram = gram - sums * (1.0 / width) * gram[ones_at : ones_at + 1, :]
    gram = jnp.concatenate([gram, jnp.zeros((80, LANES - 80), jnp.float32)], axis=1)
    gram_high = gram.astype(jnp.bfloat16)
    left_over = gram - gram_high.astype(jnp.float32)
    gram_middle = left_over.astype(jnp.bfloat16)
    gram_low = (left_over - gram_middle.astype(jnp.float32)).astype(jnp.bfloat16)
    gram_ref[...] = jnp.concatenate([gram_high, gram_middle, gram_low], axis=1)
    bias_row = centered[64:65] + centered[65:66] + centered[66:67]
    tail = lax.broadcasted_iota(jnp.int32, (8, centered.shape[1]), 0)
    mixing = jnp.concatenate(
        [centered[:64], jnp.where(tail == 0, jnp.broadcast_to(bias_row, tail.shape), 0.0)], axis=0
    )
    mixing_high = mixing.astype(jnp.bfloat16)
    mixing_low = (mixing - mixing_high.astype(jnp.float32)).astype(jnp.bfloat16)
    mixing = jnp.concatenate([mixing_high, mixing_low], axis=1)

    half = half_tiles * LANES
    side = lax.axis_index("rep") * half
    copies[8].wait()
    latent = jnp.concatenate([latent_ref[0], latent_ref[1]], axis=1)
    latent_high = latent.astype(jnp.bfloat16).astype(jnp.float32)
    latent_middle = (latent - latent_high).astype(jnp.bfloat16).astype(jnp.float32)
    latent_pieces = (latent_high, latent_middle, latent - latent_high - latent_middle)
    row = lax.broadcasted_iota(jnp.int32, (BIAS_ROWS, LANES), 0)
    for target in range(devices):
        start = columns * target // LANES * LANES
        part = up_ref[:, pl.ds(pl.multiple_of(start + side, LANES), half)]
        table = jnp.dot(
            mixing, jnp.concatenate([part, part], axis=0), preferred_element_type=jnp.float32
        )
        biases = jnp.zeros((BIAS_ROWS, LANES), jnp.float32)
        for tile in range(half_tiles):
            piece = table[:, tile * LANES : (tile + 1) * LANES]
            send_ref[target, tile * TABLE_ROWS : (tile + 1) * TABLE_ROWS, :] = piece[
                :TABLE_ROWS
            ].astype(jnp.bfloat16)
            biases = jnp.where(
                row == tile,
                jnp.broadcast_to(piece[TABLE_ROWS : TABLE_ROWS + 1], biases.shape),
                biases,
            )
        request = target % REQUESTS
        for index, piece in enumerate(latent_pieces):
            biases = jnp.where(
                row == LATENT_ROW + index,
                jnp.broadcast_to(piece[request : request + 1], biases.shape),
                biases,
            )
        send_ref[target, half_tiles * TABLE_ROWS : table_rows, :] = biases.astype(jnp.bfloat16)
        writes.append(
            pltpu.make_async_copy(
                send_ref.at[target, 0:table_rows],
                sent_ref.at[target, 0:table_rows],
                out_sems.at[1 + target],
            )
        )
        writes[-1].start()
    for write in writes:
        write.wait()


def choose_kernel(ids_ref, got_ref, out_ref):
    count = out_ref.shape[1]
    for request in range(REQUESTS):
        out_ref[request] = got_ref[ids_ref[request], 0:count, :]


def group_sum(x):
    grouped = x.reshape(x.shape[0] // 8, 8, x.shape[1])
    grouped = grouped + pltpu.roll(grouped, 2, 1)
    grouped = grouped + pltpu.roll(grouped, 4, 1)
    return grouped.reshape(x.shape)


def modulate_kernel(gate_ref, shift_ref, scale_ref, weight_ref, rows_ref, head_ref):
    width = gate_ref.shape[1]
    quarter = width // QUARTERS
    mine = lax.axis_index("seq")
    part_of_row = lax.broadcasted_iota(jnp.int32, (8, quarter), 0) // 2
    for index, ref in enumerate((gate_ref, shift_ref, scale_ref)):
        block = ref[pl.ds(pl.multiple_of(mine // 8 * 8, 8), 8), :]
        row = pltpu.roll(block, (8 - mine % 8) % 8, 0)[0:1]
        value = jnp.zeros((8, quarter), jnp.float32)
        for part in range(QUARTERS):
            piece = row[:, part * quarter : (part + 1) * quarter]
            value = jnp.where(part_of_row == part, jnp.broadcast_to(piece, value.shape), value)
        rows_ref[index] = value
    channels = weight_ref.shape[0]
    for part in range(QUARTERS):
        head_ref[part * channels : (part + 1) * channels, :] = weight_ref[
            :, part * quarter : (part + 1) * quarter
        ]


def sigma_change(position):
    now = noise_level(position.astype(jnp.float32))
    return noise_level((position + 1).astype(jnp.float32)) - now


def attend_kernel(
    lengths_ref,
    guidance_ref,
    step_ref,
    got_ref,
    rows_ref,
    head_ref,
    bias_ref,
    out_ref,
    residual_ref,
    pick_ref,
    *,
    table_rows,
):
    devices = got_ref.shape[0]
    quarter = rows_ref.shape[2]
    width = quarter * QUARTERS
    tiles = quarter // LANES
    size = devices * 8
    mine = lax.axis_index("seq")
    limit = lengths_ref[mine % REQUESTS]
    score_scale = 1.0 / HEAD_DIM**0.5

    row = lax.broadcasted_iota(jnp.int32, (size, size), 0)
    column = lax.broadcasted_iota(jnp.int32, (size, size), 1)
    key_token = column // 8 * 2 + column % 2
    allowed = (row % 8 // 2 == column % 8 // 2) & (key_token < limit)

    def modulation(index, tile):
        value = rows_ref[index, :, tile * LANES : (tile + 1) * LANES]
        return jnp.broadcast_to(value[None], (devices, 8, LANES)).reshape(size, LANES)

    total = jnp.zeros((size, LANES), jnp.float32)
    def states(kind, tile):
        first = (kind * tiles + tile) * 8
        return got_ref[:, table_rows + first : table_rows + first + 8, :].reshape(size, LANES)

    for first in range(0, tiles, TOGETHER):
        group = range(first, min(first + TOGETHER, tiles))
        scores = [
            jnp.where(allowed, nt_dot(states(0, t), states(1, t)) * score_scale, -jnp.inf)
            for t in group
        ]
        peaks = [jnp.max(x, axis=-1, keepdims=True) for x in scores]
        raised = [jnp.exp(x - peak) for x, peak in zip(scores, peaks)]
        factors = [1.0 / jnp.sum(x, axis=-1, keepdims=True) for x in raised]
        weights = [(x * factor).astype(jnp.bfloat16) for x, factor in zip(raised, factors)]
        for tile, weight in zip(group, weights):
            attended = jnp.dot(
                weight, states(2, tile), preferred_element_type=jnp.float32
            ).astype(jnp.bfloat16)
            residual = states(3, tile).astype(jnp.float32) + modulation(
                0, tile
            ) * attended.astype(jnp.float32)
            residual_ref[tile] = residual
            total = total + residual
    mean = jnp.sum(group_sum(total), axis=-1, keepdims=True) * (1.0 / width)
    total = jnp.zeros((size, LANES), jnp.float32)
    for tile in range(tiles):
        centered = residual_ref[tile] - mean
        residual_ref[tile] = centered
        total = total + centered * centered
    variance = jnp.sum(group_sum(total), axis=-1, keepdims=True) * (1.0 / width)
    inverse = lax.rsqrt(variance + 1e-06)
    channels = head_ref.shape[0] // QUARTERS
    product = jnp.zeros((size, QUARTERS * channels), jnp.float32)
    for tile in range(tiles):
        normed = residual_ref[tile] * inverse * (1.0 + modulation(2, tile)) + modulation(1, tile)
        product = product + nt_dot(
            normed.astype(jnp.bfloat16), head_ref[:, tile * LANES : (tile + 1) * LANES]
        )
    row = lax.broadcasted_iota(jnp.int32, product.shape, 0)
    column = lax.broadcasted_iota(jnp.int32, product.shape, 1)
    product = jnp.where(row % 8 // 2 == column // channels, product, 0.0)
    product = group_sum(product[:, :LANES] + product[:, LANES:])
    product = product + pltpu.roll(product, channels, 1)
    bias = bias_ref[...]
    product = product + jnp.concatenate([bias, bias], axis=1)
    pick_ref[...] = product
    first_token = pick_ref[pl.ds(0, devices, stride=8), :]
    second_token = pick_ref[pl.ds(1, devices, stride=8), :]
    lane = lax.broadcasted_iota(jnp.int32, (devices, LANES), 1)
    stream_velocity = jnp.where(lane < channels, first_token, second_token)
    pieces = got_ref[:, table_rows - BIAS_ROWS : table_rows, :].astype(jnp.float32)
    latent = sum(pieces[:, LATENT_ROW + index, :] for index in range(3))
    guidance = jnp.full((devices, LANES), guidance_ref[mine % REQUESTS], jnp.float32)
    change = sigma_change(jnp.full((devices, LANES), step_ref[mine % REQUESTS], jnp.int32))
    conditional = latent + change * guidance * stream_velocity
    unconditional = change * (1.0 - guidance) * stream_velocity
    block = jnp.where(jnp.full((devices, LANES), mine, jnp.int32) < REQUESTS, conditional, unconditional)
    out_ref[...] = jnp.broadcast_to(block[None], out_ref.shape)


def finish_kernel(
    ids_ref,
    got_ref,
    step_ref,
    own_ref,
    gram_ref,
    near_ref,
    far_ref,
    velocity_ref,
    latent_ref,
    delta_ref,
    latent_all,
    product_ref,
    *,
    devices,
    columns,
    half_tiles,
):
    block = devices
    request_row = lax.broadcasted_iota(jnp.int32, (REQUESTS, LANES), 0)
    position = jnp.zeros((REQUESTS, LANES), jnp.int32)
    for request in range(REQUESTS):
        position = jnp.where(request_row == request, step_ref[request], position)
    change = sigma_change(position)
    lane = lax.broadcasted_iota(jnp.int32, (REQUESTS, LANES), 1)
    channels = LANES // 2
    pieces = []
    for source in range(devices):
        conditional = got_ref[pl.ds(source, REQUESTS, stride=block), :]
        unconditional = got_ref[pl.ds(REQUESTS * block + source, REQUESTS, stride=block), :]
        latent_next = conditional + unconditional
        latent_all[source] = latent_next
        tail = jnp.where(lane < channels + 3, 1.0, 0.0)
        pieces.append(jnp.where(lane < channels, latent_next, tail))
        pieces.append(jnp.where(lane < channels, pltpu.roll(latent_next, channels, 1), tail))
    mine = lax.axis_index("seq")
    latent_next = latent_all[mine]
    own = jnp.concatenate([own_ref[0], own_ref[1]], axis=1)
    velocity = (latent_next - own) / change
    velocity_ref[0] = velocity[:, :channels]
    velocity_ref[1] = velocity[:, channels:]
    latent_ref[0] = latent_next[:, :channels]
    latent_ref[1] = latent_next[:, channels:]

    rounded = jnp.concatenate(pieces, axis=0).astype(jnp.bfloat16)
    rows = rounded.shape[0]
    exact = rounded.astype(jnp.float32)
    used = gram_ref.shape[0]
    pieces = jnp.dot(rounded[:, :used], gram_ref[...], preferred_element_type=jnp.float32)
    image = pieces[:, :LANES] + pieces[:, LANES : 2 * LANES] + pieces[:, 2 * LANES :]
    spread = jnp.sum(image * exact, axis=-1, keepdims=True)
    inverse = lax.rsqrt(spread * (1.0 / (HEADS * HEAD_DIM)) + 1e-06)

    row = lax.broadcasted_iota(jnp.int32, (rows, LANES), 0) % REQUESTS
    column = lax.broadcasted_iota(jnp.int32, (rows, LANES), 1)
    twice = jnp.where(column < channels, exact, pltpu.roll(exact, channels, 1))
    request_here = row - jnp.where(column < channels, 0, 1)
    left = jnp.concatenate(
        [
            jnp.where(request_here == request, twice, 0.0).astype(jnp.bfloat16)
            for request in range(0, REQUESTS, 2)
        ],
        axis=1,
    )
    half = half_tiles * LANES
    side = lax.axis_index("rep")

    def near(request, first, last):
        return near_ref[ids_ref[request], first:last, :]

    def far(request, first, last):
        return far_ref[request, first:last, :]

    bias_row = lax.broadcasted_iota(jnp.int32, (REQUESTS, LANES), 0)
    bias_at = half_tiles * TABLE_ROWS
    for which, take in ((side, near), (1 - side, far)):
        right = jnp.concatenate(
            [
                jnp.concatenate(
                    [
                        take(request, tile * TABLE_ROWS, (tile + 1) * TABLE_ROWS)
                        for request in range(REQUESTS)
                    ],
                    axis=0,
                )
                for tile in range(half_tiles)
            ],
            axis=1,
        )
        biases = [jnp.zeros((REQUESTS, LANES), jnp.float32)] * half_tiles
        for request in range(REQUESTS):
            block = take(request, bias_at, bias_at + BIAS_ROWS).astype(jnp.float32)
            biases = [
                jnp.where(bias_row == request, jnp.broadcast_to(block[t : t + 1], bias.shape), bias)
                for t, bias in enumerate(biases)
            ]
        bias = jnp.concatenate(biases, axis=1)
        product = jnp.dot(left, right, preferred_element_type=jnp.float32)
        product = product.reshape(rows // REQUESTS, REQUESTS, half) + bias[None]
        product_ref[:, pl.ds(pl.multiple_of(which * half, LANES), half)] = (
            product.reshape(rows, half) * inverse
        )
    shape = delta_ref.shape
    offsets = sorted({columns * target % LANES for target in range(devices)})
    own = columns * mine % LANES
    for offset in offsets:

        @pl.when(own == offset)
        def _(offset=offset):
            kept = product_ref[:, offset : offset + columns]
            delta_ref[...] = kept.astype(jnp.bfloat16).reshape(shape)


def broadcast(value, axis, source):
    kept = jnp.where(lax.axis_index(axis) == source, value, 0).astype(value.dtype)
    return lax.psum(kept, axis)


def noise_level(position):
    fraction = 1.0 - position / STEPS
    return 5.0 * fraction / (1.0 + 4.0 * fraction)


def layer_normed(rows):
    row_mean = jnp.mean(rows, axis=-1, keepdims=True)
    centered = rows - row_mean
    row_var = jnp.mean(centered * centered, axis=-1, keepdims=True)
    return centered * lax.rsqrt(row_var + 1e-06)


def many_per_stream(
    queries,
    key_states,
    value_states,
    hidden,
    residual_gate,
    head_shift,
    head_scale,
    head_weight,
    head_bias,
    guidance,
    step_index,
    lengths,
    latent,
    embed_weight,
    embed_bias,
    adapter_ids,
    adapter_down,
    adapter_up,
):
    row_count, stream_count, feature_width = queries.shape
    axis_devices = lax.axis_size("seq")
    full_length = row_count * axis_devices
    item_count = stream_count * feature_width // HEAD_DIM
    local_items = item_count // axis_devices
    score_scale = 1.0 / HEAD_DIM**0.5

    def as_items(states):
        return states.reshape(row_count, item_count, HEAD_DIM)

    query_heads, key_heads, value_heads = (
        lax.all_to_all(as_items(queries), "seq", split_axis=1, concat_axis=0, tiled=True),
        lax.all_to_all(as_items(key_states), "seq", split_axis=1, concat_axis=0, tiled=True),
        lax.all_to_all(as_items(value_states), "seq", split_axis=1, concat_axis=0, tiled=True),
    )
    first_item = lax.axis_index("seq") * local_items
    item_request = (first_item + jnp.arange(local_items)) // HEADS % REQUESTS
    selector = (item_request[:, None] == jnp.arange(REQUESTS)[None, :]).astype(jnp.int32)
    key_limit = jnp.sum(selector * lengths[None, :], axis=1)

    def attend(operands):
        query_rows, key_rows, value_rows, key_bound = operands
        scores = (
            jnp.einsum("qd,kd->qk", query_rows, key_rows, preferred_element_type=jnp.float32)
            * score_scale
        )
        allowed = jnp.arange(full_length)[None, :] < key_bound
        scores = jnp.where(allowed, scores, -jnp.inf)
        weights = jax.nn.softmax(scores, axis=-1).astype(jnp.bfloat16)
        return jnp.dot(weights, value_rows, preferred_element_type=jnp.float32).astype(jnp.bfloat16)

    attended_items = lax.map(
        attend,
        (
            jnp.moveaxis(query_heads, 1, 0),
            jnp.moveaxis(key_heads, 1, 0),
            jnp.moveaxis(value_heads, 1, 0),
            key_limit,
        ),
    )
    returned = lax.all_to_all(
        jnp.moveaxis(attended_items, 0, 1), "seq", split_axis=0, concat_axis=1, tiled=True
    )
    attended = returned.reshape(row_count, stream_count, feature_width)
    residual = hidden.astype(jnp.float32) + residual_gate[None, :, :] * attended.astype(jnp.float32)
    normed = (layer_normed(residual) * (1.0 + head_scale[None]) + head_shift[None]).astype(
        jnp.bfloat16
    )
    stream_velocity = jnp.dot(
        normed.reshape(-1, feature_width), head_weight, preferred_element_type=jnp.float32
    )
    stream_velocity = stream_velocity.reshape(row_count, stream_count, -1) + head_bias
    conditional = stream_velocity[:, :REQUESTS]
    unconditional = stream_velocity[:, REQUESTS:]
    velocity = unconditional + guidance[None, :, None] * (conditional - unconditional)
    sigma_now = noise_level(step_index.astype(jnp.float32))
    sigma_next = noise_level((step_index + 1).astype(jnp.float32))
    latent_next = latent + (sigma_next - sigma_now)[None, :, None] * velocity
    latent_rounded = latent_next.astype(jnp.bfloat16)
    held_slots = adapter_down.shape[0]
    embedded = jnp.dot(
        latent_rounded.reshape(row_count * REQUESTS, -1),
        embed_weight,
        preferred_element_type=jnp.float32,
    )
    embedded = embedded.reshape(row_count, REQUESTS, feature_width) + embed_bias
    block_input = layer_normed(embedded).astype(jnp.bfloat16)
    up_parts = lax.all_to_all(adapter_up, "seq", split_axis=1, concat_axis=0, tiled=True)
    user_count = up_parts.shape[0]
    chooser = (adapter_ids[:, None] == jnp.arange(user_count)[None, :]).astype(jnp.bfloat16)
    up_used = jnp.einsum(
        "ru,uck->rck", chooser, up_parts, preferred_element_type=jnp.float32
    ).astype(jnp.bfloat16)
    down_list = []
    for request in range(REQUESTS):
        owner_device = adapter_ids[request] // held_slots
        owner_slot = adapter_ids[request] % held_slots
        own_down = lax.dynamic_index_in_dim(adapter_down, owner_slot, 0, keepdims=False)
        whole_down = broadcast(own_down, "seq", owner_device)
        down_list.append(whole_down)
    down_used = jnp.stack(down_list, axis=0)
    low_rank = jnp.einsum(
        "lrd,rdk->lrk", block_input, down_used, preferred_element_type=jnp.float32
    ).astype(jnp.bfloat16)
    low_rank_all = lax.all_gather(low_rank, "seq", axis=0, tiled=True)
    adapter_delta = jnp.einsum(
        "lrk,rck->lrc", low_rank_all, up_used, preferred_element_type=jnp.float32
    ).astype(jnp.bfloat16)
    return (velocity, latent_next, adapter_delta)


def whole(shape):
    return pl.BlockSpec(shape, lambda *_: (0,) * len(shape))


def one_stream_each(
    queries,
    key_states,
    value_states,
    hidden,
    residual_gate,
    head_shift,
    head_scale,
    head_weight,
    head_bias,
    guidance,
    step_index,
    lengths,
    latent,
    embed_weight,
    embed_bias,
    adapter_ids,
    adapter_down,
    adapter_up,
):
    devices = lax.axis_size("seq")
    row_count, stream_count, width = queries.shape
    columns = adapter_up.shape[1] // devices
    half_tiles = window_tiles(columns, devices) // 2
    table_rows = half_tiles * TABLE_ROWS + BIAS_ROWS
    send_rows = table_rows + 4 * (width // QUARTERS // LANES) * 8
    swap = [(0, 1), (1, 0)]
    other_ids = lax.ppermute(adapter_ids, "rep", swap)
    smem = pl.BlockSpec(memory_space=pltpu.SMEM)
    vmem = pl.BlockSpec(memory_space=pltpu.VMEM)
    anywhere = pl.BlockSpec(memory_space=pl.ANY)
    params = pltpu.CompilerParams(vmem_limit_bytes=VMEM_LIMIT)

    sources = (
        queries,
        key_states,
        value_states,
        hidden,
        embed_weight,
        embed_bias[None, :],
        adapter_down[0].T,
        latent,
        adapter_up[0].T,
    )
    send, gram = pl.pallas_call(
        functools.partial(
            prepare_kernel, devices=devices, columns=columns, half_tiles=half_tiles
        ),
        out_shape=(
            jax.ShapeDtypeStruct((devices, send_rows, LANES), jnp.bfloat16),
            jax.ShapeDtypeStruct((80, 3 * LANES), jnp.bfloat16),
        ),
        in_specs=[anywhere] * len(sources),
        out_specs=(anywhere, vmem),
        scratch_shapes=[pltpu.VMEM(source.shape, source.dtype) for source in sources]
        + [
            pltpu.VMEM((devices, send_rows, LANES), jnp.bfloat16),
            pltpu.SemaphoreType.DMA((len(sources),)),
            pltpu.SemaphoreType.DMA((1 + devices,)),
        ],
        compiler_params=pltpu.CompilerParams(vmem_limit_bytes=PREPARE_VMEM_LIMIT),
        name="prepare",
    )(*sources)
    got = lax.all_to_all(send, "seq", split_axis=0, concat_axis=0, tiled=True)

    chosen = pl.pallas_call(
        choose_kernel,
        out_shape=jax.ShapeDtypeStruct((REQUESTS, table_rows, LANES), jnp.bfloat16),
        in_specs=[smem, vmem],
        out_specs=vmem,
        compiler_params=params,
        name="choose",
    )(other_ids, got)
    far = lax.ppermute(chosen, "rep", swap)

    quarter = width // QUARTERS
    channels = head_weight.shape[1]
    rows, head = pl.pallas_call(
        modulate_kernel,
        out_shape=(
            jax.ShapeDtypeStruct((3, 8, quarter), jnp.float32),
            jax.ShapeDtypeStruct((QUARTERS * channels, quarter), head_weight.dtype),
        ),
        in_specs=[vmem] * 4,
        out_specs=(vmem, vmem),
        compiler_params=params,
        name="modulate",
    )(residual_gate, head_shift, head_scale, head_weight.T)
    payload_rows = devices
    payload = pl.pallas_call(
        functools.partial(attend_kernel, table_rows=table_rows),
        out_shape=jax.ShapeDtypeStruct((devices, payload_rows, LANES), jnp.float32),
        in_specs=[smem] * 3 + [vmem] * 4,
        out_specs=vmem,
        scratch_shapes=[
            pltpu.VMEM((quarter // LANES, devices * 8, LANES), jnp.float32),
            pltpu.VMEM((devices * 8, LANES), jnp.float32),
        ],
        compiler_params=params,
        name="attend",
        cost_estimate=pl.CostEstimate(
            flops=10**9, bytes_accessed=4 * 10**6, transcendentals=2 * 10**5
        ),
    )(
        lengths,
        guidance,
        step_index,
        got,
        rows,
        head,
        head_bias[None, :],
    )
    shared = lax.all_to_all(payload, "seq", split_axis=0, concat_axis=0, tiled=True)

    across = (REQUESTS, LANES)
    return pl.pallas_call(
        functools.partial(finish_kernel, devices=devices, columns=columns, half_tiles=half_tiles),
        out_shape=(
            jax.ShapeDtypeStruct(latent.shape, jnp.float32),
            jax.ShapeDtypeStruct(latent.shape, jnp.float32),
            jax.ShapeDtypeStruct((row_count * devices, REQUESTS, columns), jnp.bfloat16),
        ),
        in_specs=[smem, vmem, smem] + [vmem] * 4,
        out_specs=(vmem, vmem, vmem),
        scratch_shapes=[
            pltpu.VMEM((devices,) + across, jnp.float32),
            pltpu.VMEM((row_count * devices * REQUESTS, 2 * half_tiles * LANES), jnp.float32),
        ],
        compiler_params=params,
        name="finish",
    )(
        adapter_ids,
        shared.reshape(devices * payload_rows, LANES),
        step_index,
        latent,
        gram,
        got,
        far,
    )


def window_tiles(columns, devices):
    most = max(
        pl.cdiv(columns * (d + 1), LANES) - columns * d // LANES for d in range(devices)
    )
    return (most + 1) // 2 * 2


def shards(*operands):
    queries, held, table = operands[0], operands[16], operands[17]
    row_count, stream_count, width = queries.shape
    devices = lax.axis_size("seq")
    columns = table.shape[1] // devices
    fits = (
        stream_count == devices
        and row_count == 2
        and held.shape[0] == 1
        and held.shape[2] == LANES // 2
        and lax.axis_size("rep") == 2
        and window_tiles(columns, devices) // 2 <= LATENT_ROW
        and width % (QUARTERS * LANES) == 0
        and all(
            columns * d // LANES + window_tiles(columns, devices) <= table.shape[1] // LANES
            for d in range(devices)
        )
    )
    return one_stream_each(*operands) if fits else many_per_stream(*operands)


def solution(mesh):
    placed = (
        P("seq", "rep", None),
        P("seq", "rep", None),
        P("seq", "rep", None),
        P("seq", "rep", None),
        P("rep", None),
        P("rep", None),
        P("rep", None),
        P(),
        P(),
        P("rep"),
        P("rep"),
        P("rep"),
        P("seq", "rep", None),
        P(),
        P(),
        P("rep"),
        P("seq", None, None),
        P("seq", None, None),
    )
    return jax.shard_map(
        shards,
        mesh=mesh,
        in_specs=placed,
        out_specs=(P("seq", "rep", None), P("seq", "rep", None), P(None, "rep", "seq")),
        check_vma=False,
    )
```
